32 devices in a mesh: groups: 2 (over x), space: 16 (over z, y, core).
Axes of the slice: x: 2, y: 2, z: 4, core: 2. Of those that a mesh axis runs over, the one named last changes fastest.
Arguments:
- atom_features: bfloat16 [288, 32, 256], P(('groups', 'space')), parts along dimension 0, may hold values from -6 to 6
- offsets: bfloat16 [288, 3, 32], P(('groups', 'space')), parts along dimension 0, may hold values from 0 to 1
- counts: int32 [288], P(('groups', 'space')), parts along dimension 0, may hold values from 8 to 32, as said below
- radial_weight: bfloat16 [4, 256, 256], replicated, may hold values from -0.375 to 0.375
- charge_weight: bfloat16 [256, 256], replicated, may hold values from -0.375 to 0.375
- wave_filter: float32 [4, 256], replicated, may hold values from -5 to 5
- wavevectors: int32 [3, 1024], replicated, may hold values from -4 to 25, as said below
Outputs:
- updated: bfloat16 [288, 32, 256], P(('groups', 'space')), parts along dimension 0
The draws below stay inside these ranges and needn't reach their ends.
There are 2 independent parts, one for each index of `groups`. The reference program is written for one: setup_inputs(seed, part) draws one part's arguments, and reference() takes and returns one part's arrays. A program takes and returns all parts, laid end to end along the dimension named above; an argument that names none is the same for every part. Nothing has to cross between parts.
Inputs may be any that keep to these rules, and one draw needn't show every extreme that they name: Cell c holds its atoms in its first counts[c] slots; in every draw some cell is full. `wavevectors`: the 1024 columns are distinct index triples from one half of the lattice: no column is zero or the negative of another; the first two indices lie in -4 to 4 and the third in 0 to 25, and where the third is 0 the first is above 0, or the first is 0 and the second above 0.
All inputs are finite; a program needn't handle non-finite values.
Results may differ from the reference program's by a relative error of at most 0.005.
Values may be sent and summed in bfloat16 or wider, within the bound.
A program may use at most 64 MiB of HBM per device.

```python
import math
import jax
import jax.numpy as jnp
from jax import lax

H = 256
K = 1024
NUM_BASIS = 4
CAP = 32
GRID = 3
NCELL = 144
N_SPACE = 16


def draw_counts(key, part):
    first_key, second_key = jax.random.split(jax.random.fold_in(key, 17))
    drawn_counts = jax.random.randint(first_key, (NCELL,), CAP // 4, CAP + 1)
    full_cell = jax.random.randint(second_key, (), 0, NCELL)
    return jnp.where(jnp.arange(NCELL) == full_cell, CAP, drawn_counts).astype(jnp.int32)


def draw_wavevectors(key, part):
    layer_depth = 25
    plane_count = 81
    first_key, second_key = jax.random.split(jax.random.fold_in(key, 29))
    candidate_total = 40 + layer_depth * plane_count
    forced_index = 40 + (layer_depth - 1) * plane_count
    picked = jax.random.permutation(first_key, candidate_total - 1)[:K - 1].astype(jnp.int32)
    picked = picked + (picked >= forced_index).astype(jnp.int32)
    chosen = jnp.concatenate([jnp.full((1,), forced_index, jnp.int32), picked])
    chosen = chosen[jax.random.permutation(second_key, K)]
    in_plane = chosen < 40
    remainder = chosen - 40
    layer_index = jnp.where(in_plane, 0, 1 + remainder // plane_count)
    flat_plane = jnp.where(in_plane, 41 + chosen, remainder % plane_count)
    index_x = flat_plane // 9 - 4
    index_y = flat_plane % 9 - 4
    return jnp.stack([index_x, index_y, layer_index]).astype(jnp.int32)


def level_of(rng, extent, cuts, smallest, top_value):
    loudness, own = 1.0, jax.random.fold_in(rng, 6)
    for dim, shards_of in cuts:
        heights = jnp.exp(jax.random.uniform(jax.random.fold_in(own, dim), (shards_of,), jnp.float32, smallest / len(cuts), top_value / len(cuts)))
        loudness = loudness * jnp.repeat(heights, extent[dim] // shards_of).reshape([-1 if axis == dim else 1 for axis in range(len(extent))])
    return loudness


def scatter_about(rng, shape, deviation, limit, cuts=(), held_as=jnp.bfloat16):
    level = level_of(rng, shape, cuts, -0.22, 0.18) if cuts else 1.0
    array = jax.random.normal(rng, shape, jnp.float32) * deviation * level
    return jnp.minimum(jnp.maximum(array, -limit), limit).astype(held_as)


def setup_inputs(seed: int = 0, part: int = 0) -> dict:
    seeds = jax.random.split(jax.random.key(seed), 8)
    own_keys = jax.random.split(jax.random.fold_in(seeds[7], part), 8)
    atom_features = scatter_about(own_keys[0], (NCELL, CAP, H), 1.0, 6.0, ((0, 16),))
    offsets = jnp.clip(1.0 * jax.random.uniform(own_keys[1], (NCELL, 3, CAP), jnp.float32) ** level_of(own_keys[1], (NCELL, 3, CAP), ((0, 16),), -0.2, 0.2), 0.0, 1.0).astype(jnp.bfloat16)
    counts = draw_counts(jax.random.fold_in(jax.random.fold_in(seeds[7], part), 71), part)
    radial_weight = scatter_about(seeds[3], (NUM_BASIS, H, H), H ** -0.5, 0.375)
    charge_weight = scatter_about(seeds[4], (H, H), H ** -0.5, 0.375)
    wave_filter = scatter_about(seeds[5], (NUM_BASIS, H), 1.0, 5.0, (), jnp.float32)
    wavevectors = draw_wavevectors(jax.random.fold_in(seeds[7], 71), part)
    return {"atom_features": atom_features, "offsets": offsets, "counts": counts, "radial_weight": radial_weight, "charge_weight": charge_weight, "wave_filter": wave_filter, "wavevectors": wavevectors}


CUTOFF = 1.0
block_rows = 512

def cell_geometry(near_count, cell_slots):
    columns = jnp.arange(near_count * cell_slots, dtype=jnp.int32)
    return (columns // cell_slots, columns % cell_slots)

def pair_tile(own_coords, near_coords, near_cell, near_slot, cell_index, layer_cells, basis_index, basis_count):
    own_x = cell_index // GRID
    own_y = cell_index % GRID
    layer_of = near_cell // layer_cells
    within = near_cell % layer_cells
    shift_x = ((within // GRID - own_x + 1) % GRID - 1).astype(jnp.float32)
    shift_y = ((within % GRID - own_y + 1) % GRID - 1).astype(jnp.float32)
    shift_z = (layer_of - 1).astype(jnp.float32)
    own_pos = own_coords.astype(jnp.float32)
    near_pos = near_coords.astype(jnp.float32)
    delta_x = (shift_x + near_pos[0])[None, :] - own_pos[0][:, None]
    delta_y = (shift_y + near_pos[1])[None, :] - own_pos[1][:, None]
    delta_z = (shift_z + near_pos[2])[None, :] - own_pos[2][:, None]
    radius = jnp.sqrt(delta_x * delta_x + delta_y * delta_y + delta_z * delta_z)
    smooth = jnp.where(radius < CUTOFF, 0.5 * (jnp.cos(math.pi * radius / CUTOFF) + 1.0), 0.0)
    centre = (basis_index + 0.5) * CUTOFF / basis_count
    scaled = (radius - centre) * (basis_count / CUTOFF)
    slot_ids = jnp.arange(own_pos.shape[1], dtype=jnp.int32)
    itself = (near_cell == layer_cells + cell_index)[None, :] & (near_slot[None, :] == slot_ids[:, None])
    return jnp.where(itself, 0.0, jnp.exp(-(scaled * scaled)) * smooth).astype(jnp.bfloat16)

def wave_numbers(wave_rows, layers_total):
    two_pi = 2.0 * math.pi
    wave_float = wave_rows.astype(jnp.float32)
    along_x = two_pi * wave_float[0] / GRID
    along_y = two_pi * wave_float[1] / GRID
    along_z = two_pi * wave_float[2] / layers_total
    return (along_x, along_y, along_z)

def phase_table(positions, wave_rows, layers_total):
    along_x, along_y, along_z = wave_numbers(wave_rows, layers_total)
    return positions[0][:, None] * along_x[None, :] + positions[1][:, None] * along_y[None, :] + positions[2][:, None] * along_z[None, :]

def structure_terms(positions, charges, wave_rows, layers_total):
    row_count = wave_rows.shape[1]
    feature_width = charges.shape[1]
    block_size = block_rows if row_count > block_rows and row_count % block_rows == 0 else row_count
    pieces = jnp.transpose(wave_rows.reshape(3, row_count // block_size, block_size), (1, 0, 2))

    def one_block(wave_block):
        phases = phase_table(positions, wave_block, layers_total)
        cosine = jnp.cos(phases).astype(jnp.bfloat16)
        sine_part = jnp.sin(phases).astype(jnp.bfloat16)
        real_part = lax.dot_general(cosine, charges, (((0,), (0,)), ((), ())), preferred_element_type=jnp.float32)
        imag_part = lax.dot_general(sine_part, charges, (((0,), (0,)), ((), ())), preferred_element_type=jnp.float32)
        return jnp.concatenate([real_part, imag_part], axis=1)
    return lax.map(one_block, pieces).reshape(row_count, 2 * feature_width)

def filter_rows(structure, wave_rows, layers_total, wave_filter):
    along_x, along_y, along_z = wave_numbers(wave_rows, layers_total)
    magnitude = jnp.sqrt(along_x * along_x + along_y * along_y + along_z * along_z)
    centres = 3.0 * jnp.arange(wave_filter.shape[0], dtype=jnp.float32)
    offset_k = (magnitude[:, None] - centres[None, :]) / 3.0
    basis_rows = jnp.exp(-(offset_k * offset_k))
    gain_rows = jnp.dot(basis_rows, wave_filter, precision=lax.Precision.HIGHEST, preferred_element_type=jnp.float32)
    return (structure * jnp.concatenate([gain_rows, gain_rows], axis=1)).astype(jnp.bfloat16)

def add_inverse(running, filtered, wave_rows, positions, layers_total):
    row_count = filtered.shape[0]
    feature_width = filtered.shape[1] // 2
    block_size = block_rows if row_count > block_rows and row_count % block_rows == 0 else row_count
    block_count = row_count // block_size
    factor_blocks = filtered.reshape(block_count, block_size, 2 * feature_width)
    wave_blocks = jnp.transpose(wave_rows.reshape(3, block_count, block_size), (1, 0, 2))

    def one_block(summed, block_item):
        factors, wave_block = block_item
        phases = phase_table(positions, wave_block, layers_total)
        cosine = jnp.cos(phases).astype(jnp.bfloat16)
        sine_part = jnp.sin(phases).astype(jnp.bfloat16)
        summed = summed + jnp.dot(cosine, factors[:, :feature_width], preferred_element_type=jnp.float32)
        summed = summed + jnp.dot(sine_part, factors[:, feature_width:], preferred_element_type=jnp.float32)
        return (summed, None)
    outcome = lax.scan(one_block, running, (factor_blocks, wave_blocks))
    return outcome[0]

def reference(atom_features, offsets, counts, radial_weight, charge_weight, wave_filter, wavevectors):
    layer_cells = GRID * GRID
    layers_total = N_SPACE
    total_cells = layer_cells * layers_total
    near_count = 3 * layer_cells
    slot_ids = jnp.arange(CAP, dtype=jnp.int32)
    live_mask = (slot_ids[None, :] < counts[:, None]).astype(jnp.float32)
    masked = (atom_features.astype(jnp.float32) * live_mask[:, :, None]).astype(jnp.bfloat16)
    masked_flat = masked.reshape(total_cells * CAP, H)
    values = jnp.stack([jnp.dot(masked_flat, radial_weight[basis_index], preferred_element_type=jnp.float32).astype(jnp.bfloat16) for basis_index in range(NUM_BASIS)])
    values = values.reshape(NUM_BASIS, layers_total, layer_cells * CAP, H)
    layer_offsets = offsets.reshape(layers_total, layer_cells, 3, CAP)
    near_cell, near_slot = cell_geometry(near_count, CAP)
    cell_ids = jnp.arange(layer_cells, dtype=jnp.int32)

    def layer_short(layer_index):
        below_layer = (layer_index - 1) % layers_total
        above_layer = (layer_index + 1) % layers_total
        near_offsets = jnp.concatenate([layer_offsets[below_layer], layer_offsets[layer_index], layer_offsets[above_layer]], axis=0)
        near_coords = jnp.transpose(near_offsets, (1, 0, 2)).reshape(3, near_count * CAP)
        near_values = jnp.concatenate([values[:, below_layer], values[:, layer_index], values[:, above_layer]], axis=1)

        def cell_short(cell_index):
            own_coords = layer_offsets[layer_index, cell_index]
            running = jnp.zeros((CAP, H), jnp.float32)
            for basis_index in range(NUM_BASIS):
                pair_weights = pair_tile(own_coords, near_coords, near_cell, near_slot, cell_index, layer_cells, basis_index, NUM_BASIS)
                running = running + jnp.dot(pair_weights, near_values[basis_index], preferred_element_type=jnp.float32)
            return running
        return lax.map(cell_short, cell_ids)
    short_sum = lax.map(layer_short, jnp.arange(layers_total, dtype=jnp.int32)).reshape(total_cells, CAP, H)
    cell_all = jnp.arange(total_cells, dtype=jnp.int32)
    within = cell_all % layer_cells
    base_x = (within // GRID).astype(jnp.float32)
    base_y = (within % GRID).astype(jnp.float32)
    base_z = (cell_all // layer_cells).astype(jnp.float32)
    coords = offsets.astype(jnp.float32)
    positions = jnp.stack([(base_x[:, None] + coords[:, 0, :]).reshape(-1), (base_y[:, None] + coords[:, 1, :]).reshape(-1), (base_z[:, None] + coords[:, 2, :]).reshape(-1)])
    charges = jnp.dot(masked_flat, charge_weight, preferred_element_type=jnp.float32).astype(jnp.bfloat16)
    structure = structure_terms(positions, charges, wavevectors, layers_total)
    filtered = filter_rows(structure, wavevectors, layers_total, wave_filter)
    reciprocal = add_inverse(jnp.zeros((total_cells * CAP, H), jnp.float32), filtered, wavevectors, positions, layers_total)
    short_scaled = short_sum * (1.0 / math.sqrt(CAP))
    recip_scaled = reciprocal * (1.0 / math.sqrt(total_cells * CAP * K))
    combined = atom_features.astype(jnp.float32) + short_scaled + recip_scaled.reshape(total_cells, CAP, H)
    return (live_mask[:, :, None] * combined).astype(jnp.bfloat16)
```

```python
import functools
import math

import jax
import jax.numpy as jnp
from jax import lax
from jax.experimental import pallas as pl
from jax.experimental.pallas import tpu as pltpu
from jax.sharding import PartitionSpec as P

GRID = 3
MESH = pl.DeviceIdType.MESH
COLORS = 2
F32 = jnp.float32
BF16 = jnp.bfloat16

COS_TURN = (
    0.9999999890590222,
    -19.739204499453972,
    64.93911745989816,
    -85.45013953091984,
    60.167630951184535,
    -25.96759924915613,
    6.528658162048644,
)
SIN_TURN = (
    6.283182793407032,
    -41.34141938561698,
    81.59613875538027,
    -76.57968785100171,
    41.20374363359195,
    -12.268859940903283,
)
COS_HALF_PI = tuple((-1) ** i * (math.pi / 2) ** (2 * i) / math.factorial(2 * i) for i in range(7))


def poly(coefs, x):
    total = coefs[-1] * x + coefs[-2]
    for c in coefs[-3::-1]:
        total = total * x + c
    return total


def layer_kernel(
    dims,
    masked_ref,
    geo_ref,
    gcol_ref,
    wave_ref,
    radial_ref,
    charge_ref,
    filt_ref,
    out_ref,
    halo_x,
    halo_geo,
    near_geo,
    cos_ref,
    sin_ref,
    acc_ref,
    recv_ref,
    full_ref,
    vals_ref,
    pair_ref,
    total_ref,
    halo_send,
    halo_recv,
    send_sem,
    recv_sem,
):
    n, stages, cells, slots, feats, basis, waves, scale_short, scale_recip = dims
    atoms = cells * slots
    rows = 2 * feats // n
    lanes = waves // COLORS
    me = lax.axis_index("space")
    above, below = lax.rem(me + 1, n), lax.rem(me + n - 1, n)

    bits = [(me // 2**j) % 2 for j in range(stages)]
    partners = [me + (1 - 2 * bits[j]) * 2**j for j in range(stages)]
    orders = [list(range(stages)), [0] + list(range(2, stages)) + ([1] if stages > 1 else [])]

    def lo_of(k, s):
        lo = 0
        for t in range(s):
            lo = lo + bits[orders[k][t]] * 2 ** (stages - 1 - t)
        return lo

    def keep_of(k, s):
        return lo_of(k, s) + bits[orders[k][s]] * 2 ** (stages - 1 - s)

    def give_of(k, s):
        return lo_of(k, s) + (1 - bits[orders[k][s]]) * 2 ** (stages - 1 - s)

    barrier = pltpu.get_barrier_semaphore()
    for peer in partners + [above, below]:
        pl.semaphore_signal(barrier, inc=1, device_id={"space": peer}, device_id_type=MESH)
    pl.semaphore_wait(barrier, stages + 2)

    halo = []
    for slot, peer in ((0, above), (1, below)):
        for which, src, dst in ((0, masked_ref, halo_x), (1, geo_ref, halo_geo)):
            copy = pltpu.make_async_remote_copy(
                src_ref=src,
                dst_ref=dst.at[slot],
                send_sem=halo_send.at[slot, which],
                recv_sem=halo_recv.at[slot, which],
                device_id={"space": peer},
                device_id_type=MESH,
            )
            copy.start()
            halo.append(copy)

    def scatter_copy(k, s):
        half = n >> (s + 1)
        return pltpu.make_async_remote_copy(
            src_ref=acc_ref.at[k, pl.ds(give_of(k, s), half)],
            dst_ref=recv_ref.at[k, pl.ds(n - (n >> s), half)],
            send_sem=send_sem.at[k, s],
            recv_sem=recv_sem.at[k, s],
            device_id={"space": partners[orders[k][s]]},
            device_id_type=MESH,
        )

    def gather_copy(k, s):
        half = n >> (s + 1)
        place = full_ref.at[k, pl.ds(keep_of(k, s), half)]
        return pltpu.make_async_remote_copy(
            src_ref=place,
            dst_ref=place,
            send_sem=send_sem.at[k, stages + s],
            recv_sem=recv_sem.at[k, stages + s],
            device_id={"space": partners[orders[k][s]]},
            device_id_type=MESH,
        )

    def scatter_finish(k, s):
        scatter_copy(k, s).wait()
        half = n >> (s + 1)
        keep = keep_of(k, s)
        base = n - (n >> s)
        if s < stages - 1:

            def add_one(i, carry):
                acc_ref[k, keep + i] = (
                    acc_ref[k, keep + i].astype(F32) + recv_ref[k, base + i].astype(F32)
                ).astype(BF16)
                return carry

            lax.fori_loop(0, half, add_one, 0)
            scatter_copy(k, s + 1).start()
        else:
            summed = acc_ref[k, keep].astype(F32) + recv_ref[k, base].astype(F32)
            magnitude = wave_ref[3:4, k * lanes : (k + 1) * lanes]
            weights = filt_ref[keep]
            gain = jnp.zeros((rows, lanes), F32)
            for b in range(basis):
                offset_k = (magnitude - 3.0 * b) * (1.0 / 3.0)
                gain = gain + weights[:, b : b + 1] * jnp.exp(-(offset_k * offset_k))
            full_ref[k, keep] = (summed * gain).astype(BF16)
            gather_copy(k, s).start()

    charges = jnp.dot(masked_ref[...], charge_ref[...], preferred_element_type=F32)
    charges_t = charges.T.astype(BF16)

    for k in range(COLORS):
        span = slice(k * lanes, (k + 1) * lanes)

        def table_rows(i, carry, span=span, k=k):
            at = pl.ds(pl.multiple_of(i * 16, 16), 16)
            turns = (
                gcol_ref[at, 3:4] * wave_ref[0:1, span]
                + gcol_ref[at, 4:5] * wave_ref[1:2, span]
                + gcol_ref[at, 5:6] * wave_ref[2:3, span]
            )
            u = turns - jnp.floor(turns + 0.5)
            sq = u * u
            cos_ref[k, at, :] = poly(COS_TURN, sq).astype(BF16)
            sin_ref[k, at, :] = (u * poly(SIN_TURN, sq)).astype(BF16)
            return carry

        lax.fori_loop(0, atoms // 16, table_rows, 0)
        real = jnp.dot(charges_t, cos_ref[k], preferred_element_type=F32)
        acc_ref[k, 0 : n // 2] = real.reshape(n // 2, rows, lanes).astype(BF16)
        imag = jnp.dot(charges_t, sin_ref[k], preferred_element_type=F32)
        acc_ref[k, n // 2 : n] = imag.reshape(n // 2, rows, lanes).astype(BF16)
        scatter_copy(k, 0).start()

    def near_values(source, layer):
        for b in range(basis):
            vals_ref[b, layer * atoms : (layer + 1) * atoms, :] = jnp.dot(
                source, radial_ref[b], preferred_element_type=F32
            ).astype(BF16)

    def own_values():
        near_values(masked_ref[...], 1)

    def halo_values():
        for copy in halo:
            copy.wait()
        near_values(halo_x[0], 0)
        near_values(halo_x[1], 2)
        near_geo[...] = jnp.concatenate([halo_geo[0], geo_ref[...], halo_geo[1]], axis=1)

    near = 3 * atoms
    mid = basis / 2.0
    group = 16

    def pair_rows(i, carry):
        cell = i // (slots // group)
        start = (i % (slots // group)) * group
        at = pl.ds(pl.multiple_of(i * group, group), group)
        own_x = (cell // GRID).astype(F32)
        own_y = (cell % GRID).astype(F32)
        col = lax.broadcasted_iota(jnp.int32, (1, near), 1)
        shift_x = near_geo[3:4, :] - own_x
        shift_x = jnp.where(shift_x > 1.5, shift_x - GRID, jnp.where(shift_x < -1.5, shift_x + GRID, shift_x))
        shift_y = near_geo[4:5, :] - own_y
        shift_y = jnp.where(shift_y > 1.5, shift_y - GRID, jnp.where(shift_y < -1.5, shift_y + GRID, shift_y))
        shift_z = jnp.where(col < atoms, -1.0, jnp.where(col < 2 * atoms, 0.0, 1.0)).astype(F32)
        dx = (shift_x + near_geo[0:1, :]) - gcol_ref[at, 0:1]
        dy = (shift_y + near_geo[1:2, :]) - gcol_ref[at, 1:2]
        dz = (shift_z + near_geo[2:3, :]) - gcol_ref[at, 2:3]
        sq = dx * dx + dy * dy + dz * dz
        radius = sq * lax.rsqrt(jnp.maximum(sq, 1e-30))
        half_cos = poly(COS_HALF_PI, sq)
        t = jnp.minimum(radius, 1.0) * basis - mid
        row = lax.broadcasted_iota(jnp.int32, (group, near), 0) + start
        itself = (col - (atoms + cell * slots)) == row
        used = (sq < 1.0) & jnp.logical_not(itself)
        core = jnp.where(used, jnp.exp(-(t * t)) * half_cos * half_cos, 0.0)
        grow = jnp.exp(t)
        fall = jnp.exp(-t)
        for b in range(basis):
            d2 = 2 * b + 1 - basis
            weight = core * math.exp(-(d2 * d2) / 4.0)
            if d2 != 0:
                factor = grow if d2 > 0 else fall
                power = factor
                for _ in range(abs(d2) - 1):
                    power = power * factor
                weight = weight * power
            pair_ref[b, at, :] = weight.astype(BF16)
        return carry

    steps = atoms // group

    def pair_span(part, parts):
        lax.fori_loop(part * steps // parts, (part + 1) * steps // parts, pair_rows, 0)

    def short_sum():
        short = jnp.zeros((atoms, feats), F32)
        for b in range(basis):
            short = short + jnp.dot(pair_ref[b], vals_ref[b], preferred_element_type=F32)
        total_ref[...] = short * scale_short

    tasks = [
        own_values,
        halo_values,
        functools.partial(pair_span, 0, 4),
        functools.partial(pair_span, 1, 4),
        functools.partial(pair_span, 2, 4),
        functools.partial(pair_span, 3, 4),
        short_sum,
    ]
    for s in range(stages):
        if tasks:
            tasks.pop(0)()
        for k in range(COLORS):
            scatter_finish(k, s)
    for s in range(stages - 1, -1, -1):
        if tasks:
            tasks.pop(0)()
        for k in range(COLORS):
            gather_copy(k, s).wait()
            if s:
                gather_copy(k, s - 1).start()
    for task in tasks:
        task()

    recip = jnp.zeros((atoms, feats), F32)
    for k in range(COLORS):
        for part, table in ((0, cos_ref), (1, sin_ref)):
            factors = full_ref[k, part * (n // 2) : (part + 1) * (n // 2)].reshape(feats, lanes)
            recip = recip + lax.dot_general(
                table[k], factors, (((1,), (1,)), ((), ())), preferred_element_type=F32
            )
    live = gcol_ref[:, 6:7]
    out_ref[...] = (
        masked_ref[...].astype(F32) + live * (total_ref[...] + recip * scale_recip)
    ).astype(BF16)


def local(atom_features, offsets, counts, radial_weight, charge_weight, wave_filter, wavevectors):
    cells, slots, feats = atom_features.shape
    basis = radial_weight.shape[0]
    waves = wavevectors.shape[1]
    n = lax.axis_size("space")
    layer = lax.axis_index("space")
    stages = n.bit_length() - 1
    assert n == 1 << stages and cells == GRID * GRID
    atoms = cells * slots
    rows = 2 * feats // n
    lanes = waves // COLORS

    slot_ids = jnp.arange(slots, dtype=jnp.int32)
    live = (slot_ids[None, :] < counts[:, None]).astype(F32)
    masked = (atom_features.astype(F32) * live[:, :, None]).astype(BF16).reshape(atoms, feats)
    cell_ids = jnp.arange(cells, dtype=jnp.int32)
    cell_x = jnp.broadcast_to((cell_ids // GRID).astype(F32)[:, None], (cells, slots))
    cell_y = jnp.broadcast_to((cell_ids % GRID).astype(F32)[:, None], (cells, slots))
    off = offsets.astype(F32)
    zero = jnp.zeros_like(cell_x)
    geo = jnp.stack(
        [off[:, 0], off[:, 1], off[:, 2], cell_x, cell_y, zero, zero, zero]
    ).reshape(8, atoms)
    gcol = jnp.stack(
        [
            off[:, 0],
            off[:, 1],
            off[:, 2],
            cell_x + off[:, 0],
            cell_y + off[:, 1],
            layer.astype(F32) + off[:, 2],
            live,
            zero,
        ],
        axis=-1,
    ).reshape(atoms, 8)
    index = wavevectors.astype(F32)
    turns = [index[0] / GRID, index[1] / GRID, index[2] / n]
    along = [2.0 * math.pi * t for t in turns]
    magnitude = jnp.sqrt(along[0] * along[0] + along[1] * along[1] + along[2] * along[2])
    blank = jnp.zeros_like(magnitude)
    wave_rows = jnp.stack(turns + [magnitude] + [blank] * 4)
    filt = jnp.concatenate([wave_filter.T, wave_filter.T]).reshape(n, rows, basis)

    dims = (
        n,
        stages,
        cells,
        slots,
        feats,
        basis,
        waves,
        1.0 / math.sqrt(slots),
        1.0 / math.sqrt(cells * n * slots * waves),
    )
    vmem = pl.BlockSpec(memory_space=pltpu.VMEM)
    out = pl.pallas_call(
        functools.partial(layer_kernel, dims),
        out_shape=jax.ShapeDtypeStruct((atoms, feats), BF16),
        in_specs=[vmem] * 7,
        out_specs=vmem,
        scratch_shapes=[
            pltpu.VMEM((2, atoms, feats), BF16),
            pltpu.VMEM((2, 8, atoms), F32),
            pltpu.VMEM((8, 3 * atoms), F32),
            pltpu.VMEM((COLORS, atoms, lanes), BF16),
            pltpu.VMEM((COLORS, atoms, lanes), BF16),
            pltpu.VMEM((COLORS, n, rows, lanes), BF16),
            pltpu.VMEM((COLORS, n - 1, rows, lanes), BF16),
            pltpu.VMEM((COLORS, n, rows, lanes), BF16),
            pltpu.VMEM((basis, 3 * atoms, feats), BF16),
            pltpu.VMEM((basis, atoms, 3 * atoms), BF16),
            pltpu.VMEM((atoms, feats), F32),
            pltpu.SemaphoreType.DMA((2, 2)),
            pltpu.SemaphoreType.DMA((2, 2)),
            pltpu.SemaphoreType.DMA((COLORS, 2 * stages)),
            pltpu.SemaphoreType.DMA((COLORS, 2 * stages)),
        ],
        compiler_params=pltpu.CompilerParams(collective_id=0, has_side_effects=True),
        name="ewald_layer",
    )(masked, geo, gcol, wave_rows, radial_weight, charge_weight, filt)
    return out.reshape(cells, slots, feats)


def solution(mesh):
    in_specs = (
        P(("groups", "space"), None, None),
        P(("groups", "space"), None, None),
        P(("groups", "space")),
        P(),
        P(),
        P(),
        P(),
    )
    out_specs = P(("groups", "space"), None, None)
    return jax.shard_map(local, mesh=mesh, in_specs=in_specs, out_specs=out_specs, check_vma=False)
```

```python
import functools
import math

import jax
import jax.numpy as jnp
from jax import lax
from jax.experimental import pallas as pl
from jax.experimental.pallas import tpu as pltpu
from jax.sharding import PartitionSpec as P

GRID = 3
MESH = pl.DeviceIdType.MESH
PLANS = (0, 1, 0, 1)
PARTS = 4
F32 = jnp.float32
BF16 = jnp.bfloat16

COS_TURN = (
    0.9999999890590222,
    -19.739204499453972,
    64.93911745989816,
    -85.45013953091984,
    60.167630951184535,
    -25.96759924915613,
    6.528658162048644,
)
SIN_TURN = (
    6.283182793407032,
    -41.34141938561698,
    81.59613875538027,
    -76.57968785100171,
    41.20374363359195,
    -12.268859940903283,
)
COS_HALF_PI = tuple((-1) ** i * (math.pi / 2) ** (2 * i) / math.factorial(2 * i) for i in range(7))


def poly(coefs, x):
    total = coefs[-1] * x + coefs[-2]
    for c in coefs[-3::-1]:
        total = total * x + c
    return total


def layer_kernel(
    dims,
    counts_ref,
    x_hbm,
    off_hbm,
    wave_hbm,
    charge_hbm,
    filter_hbm,
    radial_hbm,
    out_ref,
    x_ref,
    off_ref,
    wavei_ref,
    charge_ref,
    wfilt_ref,
    radial_ref,
    masked_ref,
    geo_ref,
    gcol_ref,
    wave_ref,
    filt_ref,
    halo_x,
    halo_geo,
    near_geo,
    cos_ref,
    sin_ref,
    acc_ref,
    recv_ref,
    full_ref,
    vals_ref,
    pair_ref,
    total_ref,
    load_sem,
    halo_send,
    halo_recv,
    send_sem,
    recv_sem,
):
    n, stages, cells, slots, feats, basis, waves, scale_short, scale_recip = dims
    atoms = cells * slots
    rows = 2 * feats // n
    colors = len(PLANS)
    lanes = waves // colors
    me = lax.axis_index("space")
    above, below = lax.rem(me + 1, n), lax.rem(me + n - 1, n)

    bits = [(me // 2**j) % 2 for j in range(stages)]
    partners = [me + (1 - 2 * bits[j]) * 2**j for j in range(stages)]
    plans = [list(range(stages)), [0] + list(range(2, stages)) + ([1] if stages > 1 else [])]
    orders = [plans[p] for p in PLANS]

    def lo_of(k, s):
        lo = 0
        for t in range(s):
            lo = lo + bits[orders[k][t]] * 2 ** (stages - 1 - t)
        return lo

    def keep_of(k, s):
        return lo_of(k, s) + bits[orders[k][s]] * 2 ** (stages - 1 - s)

    def give_of(k, s):
        return lo_of(k, s) + (1 - bits[orders[k][s]]) * 2 ** (stages - 1 - s)

    barrier = pltpu.get_barrier_semaphore()
    for peer in partners + [above, below]:
        pl.semaphore_signal(barrier, inc=1, device_id={"space": peer}, device_id_type=MESH)

    loads = [
        pltpu.make_async_copy(src, dst, load_sem.at[i])
        for i, (src, dst) in enumerate(
            (
                (off_hbm, off_ref),
                (x_hbm, x_ref),
                (wave_hbm, wavei_ref),
                (charge_hbm, charge_ref),
                (filter_hbm, wfilt_ref),
                (radial_hbm, radial_ref),
            )
        )
    ]
    for load in loads:
        load.start()

    lane = lax.broadcasted_iota(jnp.int32, (1, atoms), 1)
    cell = lane // slots
    held = jnp.zeros((1, atoms), jnp.int32)
    for c in range(cells):
        held = jnp.where(cell == c, counts_ref[c], held)
    live_row = jnp.where(lane % slots < held, 1.0, 0.0).astype(F32)
    cell_x = (cell // GRID).astype(F32)
    cell_y = (cell % GRID).astype(F32)
    loads[0].wait()
    off = jnp.concatenate([off_ref[c].astype(F32) for c in range(cells)], axis=1)
    geo_ref[...] = jnp.concatenate(
        [off, cell_x, cell_y, live_row, jnp.zeros((2, atoms), F32)], axis=0
    )
    placed = jnp.concatenate(
        [
            off,
            cell_x + off[0:1],
            cell_y + off[1:2],
            me.astype(F32) + off[2:3],
            live_row,
            jnp.zeros((1, atoms), F32),
        ],
        axis=0,
    )
    gcol_ref[...] = placed.T
    loads[1].wait()
    masked_ref[...] = (
        x_ref[...].reshape(atoms, feats).astype(F32) * gcol_ref[:, 6:7]
    ).astype(BF16)
    loads[2].wait()
    wave = wavei_ref[...].astype(F32)
    tx, ty, tz = wave[0:1] * (1.0 / GRID), wave[1:2] * (1.0 / GRID), wave[2:3] * (1.0 / n)
    length = (2.0 * math.pi) * jnp.sqrt(tx * tx + ty * ty + tz * tz)
    wave_ref[...] = jnp.concatenate([tx, ty, tz, length, jnp.zeros((4, waves), F32)], axis=0)

    pl.semaphore_wait(barrier, stages + 2)
    halo = []
    for slot, peer in ((0, above), (1, below)):
        for which, src, dst in ((0, masked_ref, halo_x), (1, geo_ref, halo_geo)):
            copy = pltpu.make_async_remote_copy(
                src_ref=src,
                dst_ref=dst.at[slot],
                send_sem=halo_send.at[slot, which],
                recv_sem=halo_recv.at[slot, which],
                device_id={"space": peer},
                device_id_type=MESH,
            )
            halo.append(copy)

    def scatter_copy(k, s):
        half = n >> (s + 1)
        return pltpu.make_async_remote_copy(
            src_ref=acc_ref.at[k, pl.ds(give_of(k, s), half)],
            dst_ref=recv_ref.at[k, pl.ds(n - (n >> s), half)],
            send_sem=send_sem.at[k, s],
            recv_sem=recv_sem.at[k, s],
            device_id={"space": partners[orders[k][s]]},
            device_id_type=MESH,
        )

    def gather_copy(k, s):
        half = n >> (s + 1)
        place = full_ref.at[k, pl.ds(keep_of(k, s), half)]
        return pltpu.make_async_remote_copy(
            src_ref=place,
            dst_ref=place,
            send_sem=send_sem.at[k, stages + s],
            recv_sem=recv_sem.at[k, stages + s],
            device_id={"space": partners[orders[k][s]]},
            device_id_type=MESH,
        )

    def scatter_finish(k, s):
        scatter_copy(k, s).wait()
        half = n >> (s + 1)
        keep = keep_of(k, s)
        base = n - (n >> s)
        if s < stages - 1:

            def add_one(i, carry):
                acc_ref[k, keep + i] = (
                    acc_ref[k, keep + i].astype(F32) + recv_ref[k, base + i].astype(F32)
                ).astype(BF16)
                return carry

            lax.fori_loop(0, half, add_one, 0)
            scatter_copy(k, s + 1).start()
        else:
            summed = acc_ref[k, keep].astype(F32) + recv_ref[k, base].astype(F32)
            magnitude = wave_ref[3:4, k * lanes : (k + 1) * lanes]
            weights = filt_ref[keep]
            gain = jnp.zeros((rows, lanes), F32)
            for b in range(basis):
                offset_k = (magnitude - 3.0 * b) * (1.0 / 3.0)
                gain = gain + weights[:, b : b + 1] * jnp.exp(-(offset_k * offset_k))
            full_ref[k, keep] = (summed * gain).astype(BF16)
            gather_copy(k, s).start()

    def inverse(k):
        recip = jnp.zeros((atoms, feats), F32)
        for part, table in ((0, cos_ref), (1, sin_ref)):
            factors = full_ref[k, part * (n // 2) : (part + 1) * (n // 2)].reshape(feats, lanes)
            recip = recip + lax.dot_general(
                table[k], factors, (((1,), (1,)), ((), ())), preferred_element_type=F32
            )
        total_ref[...] = total_ref[...] + recip * scale_recip

    def exchange(k, step):
        if step < stages:
            scatter_finish(k, step)
        else:
            s = 2 * stages - 1 - step
            gather_copy(k, s).wait()
            if s:
                gather_copy(k, s - 1).start()

    loads[3].wait()
    charges = jnp.dot(masked_ref[...], charge_ref[...], preferred_element_type=F32)
    charges_t = charges.T.astype(BF16)

    def tables(k):
        span = slice(k * lanes, (k + 1) * lanes)

        def table_rows(i, carry):
            at = pl.ds(pl.multiple_of(i * 32, 32), 32)
            turns = (
                gcol_ref[at, 3:4] * wave_ref[0:1, span]
                + gcol_ref[at, 4:5] * wave_ref[1:2, span]
                + gcol_ref[at, 5:6] * wave_ref[2:3, span]
            )
            u = turns - jnp.floor(turns + 0.5)
            sq = u * u
            cos_ref[k, at, :] = poly(COS_TURN, sq).astype(BF16)
            sin_ref[k, at, :] = (u * poly(SIN_TURN, sq)).astype(BF16)
            return carry

        lax.fori_loop(0, atoms // 32, table_rows, 0)
        real = jnp.dot(charges_t, cos_ref[k], preferred_element_type=F32)
        acc_ref[k, 0 : n // 2] = real.reshape(n // 2, rows, lanes).astype(BF16)
        imag = jnp.dot(charges_t, sin_ref[k], preferred_element_type=F32)
        acc_ref[k, n // 2 : n] = imag.reshape(n // 2, rows, lanes).astype(BF16)
        scatter_copy(k, 0).start()

    def near_values(source, layer):
        for b in range(basis):
            vals_ref[b, layer * atoms : (layer + 1) * atoms, :] = jnp.dot(
                source, radial_ref[b], preferred_element_type=F32
            ).astype(BF16)

    def own_values():
        loads[4].wait()
        loads[5].wait()
        wide = filt_ref.shape[-1]
        weights = jnp.concatenate(
            [wfilt_ref[...], jnp.zeros((wide - basis, feats), F32)], axis=0
        ).T.reshape(n // 2, rows, wide)
        filt_ref[0 : n // 2] = weights
        filt_ref[n // 2 : n] = weights
        near_values(masked_ref[...], 1)

    def halo_values():
        for copy in halo:
            copy.wait()
        near_values(halo_x[0], 0)
        near_values(halo_x[1], 2)
        near_geo[...] = jnp.concatenate([halo_geo[0], geo_ref[...], halo_geo[1]], axis=1)

    near = 3 * atoms
    mid = basis / 2.0
    group = 16

    def pair_rows(i, carry):
        cell = i // (slots // group)
        start = (i % (slots // group)) * group
        at = pl.ds(pl.multiple_of(i * group, group), group)
        own_x = (cell // GRID).astype(F32)
        own_y = (cell % GRID).astype(F32)
        col = lax.broadcasted_iota(jnp.int32, (1, near), 1)
        shift_x = near_geo[3:4, :] - own_x
        shift_x = jnp.where(shift_x > 1.5, shift_x - GRID, jnp.where(shift_x < -1.5, shift_x + GRID, shift_x))
        shift_y = near_geo[4:5, :] - own_y
        shift_y = jnp.where(shift_y > 1.5, shift_y - GRID, jnp.where(shift_y < -1.5, shift_y + GRID, shift_y))
        shift_z = jnp.where(col < atoms, -1.0, jnp.where(col < 2 * atoms, 0.0, 1.0)).astype(F32)
        dx = (shift_x + near_geo[0:1, :]) - gcol_ref[at, 0:1]
        dy = (shift_y + near_geo[1:2, :]) - gcol_ref[at, 1:2]
        dz = (shift_z + near_geo[2:3, :]) - gcol_ref[at, 2:3]
        sq = dx * dx + dy * dy + dz * dz
        radius = sq * lax.rsqrt(jnp.maximum(sq, 1e-30))
        half_cos = poly(COS_HALF_PI, sq)
        t = jnp.minimum(radius, 1.0) * basis - mid
        row = lax.broadcasted_iota(jnp.int32, (group, near), 0) + start
        itself = (col - (atoms + cell * slots)) == row
        used = (sq < 1.0) & jnp.logical_not(itself)
        core = jnp.where(used, jnp.exp(-(t * t)) * half_cos * half_cos, 0.0)
        grow = jnp.exp(t)
        fall = jnp.exp(-t)
        for b in range(basis):
            d2 = 2 * b + 1 - basis
            weight = core * math.exp(-(d2 * d2) / 4.0)
            if d2 != 0:
                factor = grow if d2 > 0 else fall
                power = factor
                for _ in range(abs(d2) - 1):
                    power = power * factor
                weight = weight * power
            pair_ref[b, at, :] = weight.astype(BF16)
        return carry

    steps = atoms // group

    def pair_span(part, parts):
        lax.fori_loop(part * steps // parts, (part + 1) * steps // parts, pair_rows, 0)

    def short_sum():
        short = jnp.zeros((atoms, feats), F32)
        for b in range(basis):
            short = short + jnp.dot(pair_ref[b], vals_ref[b], preferred_element_type=F32)
        total_ref[...] = short * scale_short

    for k in range(colors):
        tables(k)
        if k == 0:
            for copy in halo:
                copy.start()
        for j in range(k):
            exchange(j, k - 1 - j)

    tasks = [own_values, halo_values]
    tasks += [functools.partial(pair_span, part, PARTS) for part in range(PARTS)] + [short_sum]
    done = [colors - 1 - j for j in range(colors)]
    while any(step < 2 * stages for step in done):
        if tasks:
            tasks.pop(0)()
        for k in range(colors):
            if done[k] < 2 * stages:
                exchange(k, done[k])
                done[k] += 1
                if done[k] == 2 * stages:
                    while tasks:
                        tasks.pop(0)()
                    inverse(k)

    out_ref[...] = (
        (masked_ref[...].astype(F32) + gcol_ref[:, 6:7] * total_ref[...])
        .astype(BF16)
        .reshape(cells, slots, feats)
    )


def local(atom_features, offsets, counts, radial_weight, charge_weight, wave_filter, wavevectors):
    cells, slots, feats = atom_features.shape
    basis = radial_weight.shape[0]
    waves = wavevectors.shape[1]
    n = lax.axis_size("space")
    stages = n.bit_length() - 1
    assert n == 1 << stages and cells == GRID * GRID
    atoms = cells * slots
    rows = 2 * feats // n
    colors = len(PLANS)
    lanes = waves // colors
    dims = (
        n,
        stages,
        cells,
        slots,
        feats,
        basis,
        waves,
        1.0 / math.sqrt(slots),
        1.0 / math.sqrt(cells * n * slots * waves),
    )
    anyspace = pl.BlockSpec(memory_space=pl.ANY)
    args = (counts, atom_features, offsets, wavevectors, charge_weight, wave_filter, radial_weight)
    return pl.pallas_call(
        functools.partial(layer_kernel, dims),
        out_shape=jax.ShapeDtypeStruct((cells, slots, feats), BF16),
        in_specs=[pl.BlockSpec(memory_space=pltpu.SMEM)] + [anyspace] * 6,
        out_specs=pl.BlockSpec(memory_space=pltpu.VMEM),
        scratch_shapes=[
            pltpu.VMEM(atom_features.shape, BF16),
            pltpu.VMEM(offsets.shape, BF16),
            pltpu.VMEM(wavevectors.shape, jnp.int32),
            pltpu.VMEM(charge_weight.shape, BF16),
            pltpu.VMEM(wave_filter.shape, F32),
            pltpu.VMEM(radial_weight.shape, BF16),
            pltpu.VMEM((atoms, feats), BF16),
            pltpu.VMEM((8, atoms), F32),
            pltpu.VMEM((atoms, 8), F32),
            pltpu.VMEM((8, waves), F32),
            pltpu.VMEM((n, rows, basis + -basis % 8), F32),
            pltpu.VMEM((2, atoms, feats), BF16),
            pltpu.VMEM((2, 8, atoms), F32),
            pltpu.VMEM((8, 3 * atoms), F32),
            pltpu.VMEM((colors, atoms, lanes), BF16),
            pltpu.VMEM((colors, atoms, lanes), BF16),
            pltpu.VMEM((colors, n, rows, lanes), BF16),
            pltpu.VMEM((colors, n - 1, rows, lanes), BF16),
            pltpu.VMEM((colors, n, rows, lanes), BF16),
            pltpu.VMEM((basis, 3 * atoms, feats), BF16),
            pltpu.VMEM((basis, atoms, 3 * atoms), BF16),
            pltpu.VMEM((atoms, feats), F32),
            pltpu.SemaphoreType.DMA((6,)),
            pltpu.SemaphoreType.DMA((2, 2)),
            pltpu.SemaphoreType.DMA((2, 2)),
            pltpu.SemaphoreType.DMA((colors, 2 * stages)),
            pltpu.SemaphoreType.DMA((colors, 2 * stages)),
        ],
        compiler_params=pltpu.CompilerParams(collective_id=0, has_side_effects=True),
        name="ewald_layer",
    )(*args)


def solution(mesh):
    in_specs = (
        P(("groups", "space"), None, None),
        P(("groups", "space"), None, None),
        P(("groups", "space")),
        P(),
        P(),
        P(),
        P(),
    )
    out_specs = P(("groups", "space"), None, None)
    return jax.shard_map(local, mesh=mesh, in_specs=in_specs, out_specs=out_specs, check_vma=False)
```

```python
import functools
import math

import jax
import jax.numpy as jnp
from jax import lax
from jax.experimental import pallas as pl
from jax.experimental.pallas import tpu as pltpu
from jax.sharding import PartitionSpec as P

GRID = 3
MESH = pl.DeviceIdType.MESH
PLANS = (1, 0)
PARTS = 4
F32 = jnp.float32
BF16 = jnp.bfloat16

COS_TURN = (
    0.9999999890590222,
    -19.739204499453972,
    64.93911745989816,
    -85.45013953091984,
    60.167630951184535,
    -25.96759924915613,
    6.528658162048644,
)
SIN_TURN = (
    6.283182793407032,
    -41.34141938561698,
    81.59613875538027,
    -76.57968785100171,
    41.20374363359195,
    -12.268859940903283,
)
COS_HALF_PI = tuple((-1) ** i * (math.pi / 2) ** (2 * i) / math.factorial(2 * i) for i in range(7))


def poly(coefs, x):
    total = coefs[-1] * x + coefs[-2]
    for c in coefs[-3::-1]:
        total = total * x + c
    return total


def layer_kernel(
    dims,
    counts_ref,
    x_hbm,
    off_hbm,
    wave_hbm,
    charge_hbm,
    filter_hbm,
    radial_hbm,
    out_ref,
    x_ref,
    off_ref,
    wavei_ref,
    charge_ref,
    wfilt_ref,
    radial_ref,
    masked_ref,
    geo_ref,
    gcol_ref,
    wave_ref,
    filt_ref,
    halo_x,
    halo_geo,
    near_geo,
    cos_ref,
    sin_ref,
    acc_ref,
    recv_ref,
    full_ref,
    vals_ref,
    pair_ref,
    total_ref,
    load_sem,
    halo_send,
    halo_recv,
    send_sem,
    recv_sem,
):
    n, widths, cells, slots, feats, basis, waves, scale_short, scale_recip = dims
    atoms = cells * slots
    rows = 2 * feats // n
    colors = len(PLANS)
    lanes = waves // colors
    me = lax.axis_index("space")
    above, below = lax.rem(me + 1, n), lax.rem(me + n - 1, n)

    stages = len(widths)
    bases = [math.prod(widths[:j]) for j in range(stages)]
    digits = [(me // bases[j]) % widths[j] for j in range(stages)]
    partners = [
        [me + ((digits[j] + d) % widths[j] - digits[j]) * bases[j] for d in range(1, widths[j])]
        for j in range(stages)
    ]
    plans = [list(range(stages)), [0] + list(range(2, stages)) + ([1] if stages > 1 else [])]
    orders = [plans[p] for p in PLANS]

    def size_of(k, s):
        size = n
        for t in range(s):
            size = size // widths[orders[k][t]]
        return size

    def lo_of(k, s):
        lo = 0
        for t in range(s):
            lo = lo + digits[orders[k][t]] * size_of(k, t + 1)
        return lo

    barrier = pltpu.get_barrier_semaphore()
    peers = [peer for group_of in partners for peer in group_of] + [above, below]
    for peer in peers:
        pl.semaphore_signal(barrier, inc=1, device_id={"space": peer}, device_id_type=MESH)

    loads = [
        pltpu.make_async_copy(src, dst, load_sem.at[i])
        for i, (src, dst) in enumerate(
            (
                (off_hbm, off_ref),
                (x_hbm, x_ref),
                (wave_hbm, wavei_ref),
                (charge_hbm, charge_ref),
                (filter_hbm, wfilt_ref),
                (radial_hbm, radial_ref),
            )
        )
    ]
    for load in loads:
        load.start()

    lane = lax.broadcasted_iota(jnp.int32, (1, atoms), 1)
    cell = lane // slots
    held = jnp.zeros((1, atoms), jnp.int32)
    for c in range(cells):
        held = jnp.where(cell == c, counts_ref[c], held)
    live_row = jnp.where(lane % slots < held, 1.0, 0.0).astype(F32)
    cell_x = (cell // GRID).astype(F32)
    cell_y = (cell % GRID).astype(F32)
    loads[0].wait()
    off = jnp.concatenate([off_ref[c].astype(F32) for c in range(cells)], axis=1)
    geo_ref[...] = jnp.concatenate(
        [off, cell_x, cell_y, live_row, jnp.zeros((2, atoms), F32)], axis=0
    )
    placed = jnp.concatenate(
        [
            off,
            cell_x + off[0:1],
            cell_y + off[1:2],
            me.astype(F32) + off[2:3],
            live_row,
            jnp.zeros((1, atoms), F32),
        ],
        axis=0,
    )
    gcol_ref[...] = placed.T
    loads[1].wait()
    masked_ref[...] = (
        x_ref[...].reshape(atoms, feats).astype(F32) * gcol_ref[:, 6:7]
    ).astype(BF16)
    loads[2].wait()
    wave = wavei_ref[...].astype(F32)
    tx, ty, tz = wave[0:1] * (1.0 / GRID), wave[1:2] * (1.0 / GRID), wave[2:3] * (1.0 / n)
    length = (2.0 * math.pi) * jnp.sqrt(tx * tx + ty * ty + tz * tz)
    wave_ref[...] = jnp.concatenate([tx, ty, tz, length, jnp.zeros((4, waves), F32)], axis=0)

    pl.semaphore_wait(barrier, len(peers))
    halo = []
    for slot, peer in ((0, above), (1, below)):
        for which, src, dst in ((0, masked_ref, halo_x), (1, geo_ref, halo_geo)):
            copy = pltpu.make_async_remote_copy(
                src_ref=src,
                dst_ref=dst.at[slot],
                send_sem=halo_send.at[slot, which],
                recv_sem=halo_recv.at[slot, which],
                device_id={"space": peer},
                device_id_type=MESH,
            )
            halo.append(copy)

    def scatter_copies(k, s):
        digit = orders[k][s]
        part = size_of(k, s + 1)
        base = n - size_of(k, s)
        return [
            pltpu.make_async_remote_copy(
                src_ref=acc_ref.at[
                    k, pl.ds(lo_of(k, s) + (digits[digit] + d) % widths[digit] * part, part)
                ],
                dst_ref=recv_ref.at[k, pl.ds(base + (d - 1) * part, part)],
                send_sem=send_sem.at[k, s, d - 1],
                recv_sem=recv_sem.at[k, s, d - 1],
                device_id={"space": partners[digit][d - 1]},
                device_id_type=MESH,
            )
            for d in range(1, widths[digit])
        ]

    def gather_copies(k, s):
        digit = orders[k][s]
        part = size_of(k, s + 1)
        place = full_ref.at[k, pl.ds(lo_of(k, s + 1), part)]
        return [
            pltpu.make_async_remote_copy(
                src_ref=place,
                dst_ref=place,
                send_sem=send_sem.at[k, stages + s, d - 1],
                recv_sem=recv_sem.at[k, stages + s, d - 1],
                device_id={"space": partners[digit][d - 1]},
                device_id_type=MESH,
            )
            for d in range(1, widths[digit])
        ]

    def start_all(copies):
        for copy in copies:
            copy.start()

    def wait_all(copies):
        for copy in copies:
            copy.wait()

    def scatter_finish(k, s):
        wait_all(scatter_copies(k, s))
        part = size_of(k, s + 1)
        keep = lo_of(k, s + 1)
        base = n - size_of(k, s)
        others = widths[orders[k][s]] - 1

        def sum_of(i):
            total = acc_ref[k, keep + i].astype(F32)
            for d in range(others):
                total = total + recv_ref[k, base + d * part + i].astype(F32)
            return total

        if s < stages - 1:

            def add_one(i, carry):
                acc_ref[k, keep + i] = sum_of(i).astype(BF16)
                return carry

            lax.fori_loop(0, part, add_one, 0)
            start_all(scatter_copies(k, s + 1))
        else:
            summed = sum_of(0)
            magnitude = wave_ref[3:4, k * lanes : (k + 1) * lanes]
            weights = filt_ref[keep]
            gain = jnp.zeros((rows, lanes), F32)
            for b in range(basis):
                offset_k = (magnitude - 3.0 * b) * (1.0 / 3.0)
                gain = gain + weights[:, b : b + 1] * jnp.exp(-(offset_k * offset_k))
            full_ref[k, keep] = (summed * gain).astype(BF16)
            start_all(gather_copies(k, s))

    def inverse(k):
        recip = jnp.zeros((atoms, feats), F32)
        for part, table in ((0, cos_ref), (1, sin_ref)):
            factors = full_ref[k, part * (n // 2) : (part + 1) * (n // 2)].reshape(feats, lanes)
            recip = recip + lax.dot_general(
                table[k], factors, (((1,), (1,)), ((), ())), preferred_element_type=F32
            )
        total_ref[...] = total_ref[...] + recip * scale_recip

    def exchange(k, step):
        if step < stages:
            scatter_finish(k, step)
        else:
            s = 2 * stages - 1 - step
            wait_all(gather_copies(k, s))
            if s:
                start_all(gather_copies(k, s - 1))

    loads[3].wait()
    charges = jnp.dot(masked_ref[...], charge_ref[...], preferred_element_type=F32)
    charges_t = charges.T.astype(BF16)

    def tables(k, between):
        span = slice(k * lanes, (k + 1) * lanes)

        def table_rows(i, carry):
            at = pl.ds(pl.multiple_of(i * 32, 32), 32)
            turns = (
                gcol_ref[at, 3:4] * wave_ref[0:1, span]
                + gcol_ref[at, 4:5] * wave_ref[1:2, span]
                + gcol_ref[at, 5:6] * wave_ref[2:3, span]
            )
            u = turns - jnp.floor(turns + 0.5)
            sq = u * u
            cos_ref[k, at, :] = poly(COS_TURN, sq).astype(BF16)
            sin_ref[k, at, :] = (u * poly(SIN_TURN, sq)).astype(BF16)
            return carry

        lax.fori_loop(0, atoms // 32, table_rows, 0)
        between()
        real = jnp.dot(charges_t, cos_ref[k], preferred_element_type=F32)
        acc_ref[k, 0 : n // 2] = real.reshape(n // 2, rows, lanes).astype(BF16)
        imag = jnp.dot(charges_t, sin_ref[k], preferred_element_type=F32)
        acc_ref[k, n // 2 : n] = imag.reshape(n // 2, rows, lanes).astype(BF16)
        start_all(scatter_copies(k, 0))

    def near_values(source, layer):
        for b in range(basis):
            vals_ref[b, layer * atoms : (layer + 1) * atoms, :] = jnp.dot(
                source, radial_ref[b], preferred_element_type=F32
            ).astype(BF16)

    def own_values():
        loads[4].wait()
        loads[5].wait()
        wide = filt_ref.shape[-1]
        weights = jnp.concatenate(
            [wfilt_ref[...], jnp.zeros((wide - basis, feats), F32)], axis=0
        ).T.reshape(n // 2, rows, wide)
        filt_ref[0 : n // 2] = weights
        filt_ref[n // 2 : n] = weights
        near_values(masked_ref[...], 1)

    def halo_places():
        wait_all(halo[1::2])
        near_geo[...] = jnp.concatenate([halo_geo[0], geo_ref[...], halo_geo[1]], axis=1)

    def halo_values():
        wait_all(halo[0::2])
        near_values(halo_x[0], 0)
        near_values(halo_x[1], 2)

    near = 3 * atoms
    mid = basis / 2.0
    group = 16

    def pair_rows(i, carry):
        cell = i // (slots // group)
        start = (i % (slots // group)) * group
        at = pl.ds(pl.multiple_of(i * group, group), group)
        own_x = (cell // GRID).astype(F32)
        own_y = (cell % GRID).astype(F32)
        col = lax.broadcasted_iota(jnp.int32, (1, near), 1)
        shift_x = near_geo[3:4, :] - own_x
        shift_x = jnp.where(shift_x > 1.5, shift_x - GRID, jnp.where(shift_x < -1.5, shift_x + GRID, shift_x))
        shift_y = near_geo[4:5, :] - own_y
        shift_y = jnp.where(shift_y > 1.5, shift_y - GRID, jnp.where(shift_y < -1.5, shift_y + GRID, shift_y))
        shift_z = jnp.where(col < atoms, -1.0, jnp.where(col < 2 * atoms, 0.0, 1.0)).astype(F32)
        dx = (shift_x + near_geo[0:1, :]) - gcol_ref[at, 0:1]
        dy = (shift_y + near_geo[1:2, :]) - gcol_ref[at, 1:2]
        dz = (shift_z + near_geo[2:3, :]) - gcol_ref[at, 2:3]
        sq = dx * dx + dy * dy + dz * dz
        radius = sq * lax.rsqrt(jnp.maximum(sq, 1e-30))
        half_cos = poly(COS_HALF_PI, sq)
        t = jnp.minimum(radius, 1.0) * basis - mid
        row = lax.broadcasted_iota(jnp.int32, (group, near), 0) + start
        itself = (col - (atoms + cell * slots)) == row
        used = (sq < 1.0) & jnp.logical_not(itself)
        core = jnp.where(used, jnp.exp(-(t * t)) * half_cos * half_cos, 0.0)
        grow = jnp.exp(t)
        fall = jnp.exp(-t)
        for b in range(basis):
            d2 = 2 * b + 1 - basis
            weight = core * math.exp(-(d2 * d2) / 4.0)
            if d2 != 0:
                factor = grow if d2 > 0 else fall
                power = factor
                for _ in range(abs(d2) - 1):
                    power = power * factor
                weight = weight * power
            pair_ref[b, at, :] = weight.astype(BF16)
        return carry

    steps = atoms // group

    def pair_span(part, parts):
        lax.fori_loop(part * steps // parts, (part + 1) * steps // parts, pair_rows, 0)

    def short_sum():
        short = jnp.zeros((atoms, feats), F32)
        for b in range(basis):
            short = short + jnp.dot(pair_ref[b], vals_ref[b], preferred_element_type=F32)
        total_ref[...] = short * scale_short

    start_all(halo[1::2])
    for k in range(colors):
        tables(k, functools.partial(exchange, k - 1, 0) if k else lambda: None)
    exchange(colors - 1, 0)

    spans = [functools.partial(pair_span, part, PARTS) for part in range(PARTS)]
    tasks = {1: [own_values, halo_places] + spans[:2], 2: spans[2:]}
    tasks[stages] = tasks.get(stages, []) + [halo_values]
    tasks[stages + 1] = tasks.get(stages + 1, []) + [short_sum]
    for step in range(1, 2 * stages):
        if step == 2:
            start_all(halo[0::2])
        for task in tasks.get(step, []):
            task()
        order = range(colors - 1, -1, -1) if step == 1 else range(colors)
        for k in order:
            exchange(k, step)
            if step == 2 * stages - 1:
                inverse(k)

    out_ref[...] = (
        (masked_ref[...].astype(F32) + gcol_ref[:, 6:7] * total_ref[...])
        .astype(BF16)
        .reshape(cells, slots, feats)
    )


def local(atom_features, offsets, counts, radial_weight, charge_weight, wave_filter, wavevectors):
    cells, slots, feats = atom_features.shape
    basis = radial_weight.shape[0]
    waves = wavevectors.shape[1]
    n = lax.axis_size("space")
    power = n.bit_length() - 1
    assert n == 1 << power and power >= 3 and cells == GRID * GRID
    widths = (2,) + (2,) * ((power - 1) % 2) + (4,) * ((power - 1) // 2)
    stages = len(widths)
    atoms = cells * slots
    rows = 2 * feats // n
    colors = len(PLANS)
    lanes = waves // colors
    dims = (
        n,
        widths,
        cells,
        slots,
        feats,
        basis,
        waves,
        1.0 / math.sqrt(slots),
        1.0 / math.sqrt(cells * n * slots * waves),
    )
    anyspace = pl.BlockSpec(memory_space=pl.ANY)
    args = (counts, atom_features, offsets, wavevectors, charge_weight, wave_filter, radial_weight)
    return pl.pallas_call(
        functools.partial(layer_kernel, dims),
        out_shape=jax.ShapeDtypeStruct((cells, slots, feats), BF16),
        in_specs=[pl.BlockSpec(memory_space=pltpu.SMEM)] + [anyspace] * 6,
        out_specs=pl.BlockSpec(memory_space=pltpu.VMEM),
        scratch_shapes=[
            pltpu.VMEM(atom_features.shape, BF16),
            pltpu.VMEM(offsets.shape, BF16),
            pltpu.VMEM(wavevectors.shape, jnp.int32),
            pltpu.VMEM(charge_weight.shape, BF16),
            pltpu.VMEM(wave_filter.shape, F32),
            pltpu.VMEM(radial_weight.shape, BF16),
            pltpu.VMEM((atoms, feats), BF16),
            pltpu.VMEM((8, atoms), F32),
            pltpu.VMEM((atoms, 8), F32),
            pltpu.VMEM((8, waves), F32),
            pltpu.VMEM((n, rows, basis + -basis % 8), F32),
            pltpu.VMEM((2, atoms, feats), BF16),
            pltpu.VMEM((2, 8, atoms), F32),
            pltpu.VMEM((8, 3 * atoms), F32),
            pltpu.VMEM((colors, atoms, lanes), BF16),
            pltpu.VMEM((colors, atoms, lanes), BF16),
            pltpu.VMEM((colors, n, rows, lanes), BF16),
            pltpu.VMEM((colors, n - 1, rows, lanes), BF16),
            pltpu.VMEM((colors, n, rows, lanes), BF16),
            pltpu.VMEM((basis, 3 * atoms, feats), BF16),
            pltpu.VMEM((basis, atoms, 3 * atoms), BF16),
            pltpu.VMEM((atoms, feats), F32),
            pltpu.SemaphoreType.DMA((6,)),
            pltpu.SemaphoreType.DMA((2, 2)),
            pltpu.SemaphoreType.DMA((2, 2)),
            pltpu.SemaphoreType.DMA((colors, 2 * stages, max(widths) - 1)),
            pltpu.SemaphoreType.DMA((colors, 2 * stages, max(widths) - 1)),
        ],
        compiler_params=pltpu.CompilerParams(collective_id=0, has_side_effects=True),
        name="ewald_layer",
    )(*args)


def solution(mesh):
    in_specs = (
        P(("groups", "space"), None, None),
        P(("groups", "space"), None, None),
        P(("groups", "space")),
        P(),
        P(),
        P(),
        P(),
    )
    out_specs = P(("groups", "space"), None, None)
    return jax.shard_map(local, mesh=mesh, in_specs=in_specs, out_specs=out_specs, check_vma=False)
```

```python
import functools
import math

import jax
import jax.numpy as jnp
from jax import lax
from jax.experimental import pallas as pl
from jax.experimental.pallas import tpu as pltpu
from jax.sharding import PartitionSpec as P

GRID = 3
MESH = pl.DeviceIdType.MESH
PLANS = (1, 0)
PARTS = 4
F32 = jnp.float32
BF16 = jnp.bfloat16

COS_TURN = (
    0.9999999890590222,
    -19.739204499453972,
    64.93911745989816,
    -85.45013953091984,
    60.167630951184535,
    -25.96759924915613,
    6.528658162048644,
)
SIN_TURN = (
    6.283182793407032,
    -41.34141938561698,
    81.59613875538027,
    -76.57968785100171,
    41.20374363359195,
    -12.268859940903283,
)
COS_HALF_PI = tuple((-1) ** i * (math.pi / 2) ** (2 * i) / math.factorial(2 * i) for i in range(7))


def poly(coefs, x):
    total = coefs[-1] * x + coefs[-2]
    for c in coefs[-3::-1]:
        total = total * x + c
    return total


def layer_kernel(
    dims,
    counts_ref,
    x_hbm,
    off_hbm,
    wave_hbm,
    charge_hbm,
    filter_hbm,
    radial_hbm,
    out_ref,
    x_ref,
    off_ref,
    wavei_ref,
    charge_ref,
    wfilt_ref,
    radial_ref,
    masked_ref,
    geo_ref,
    gcol_ref,
    wave_ref,
    filt_ref,
    halo_x,
    halo_geo,
    near_geo,
    cos_ref,
    sin_ref,
    acc_ref,
    recv_ref,
    full_ref,
    vals_ref,
    pair_ref,
    total_ref,
    load_sem,
    halo_send,
    halo_recv,
    send_sem,
    recv_sem,
):
    n, widths, cells, slots, feats, basis, waves, scale_short, scale_recip = dims
    atoms = cells * slots
    rows = 2 * feats // n
    colors = len(PLANS)
    lanes = waves // colors
    me = lax.axis_index("space")
    above, below = lax.rem(me + 1, n), lax.rem(me + n - 1, n)

    stages = len(widths)
    bases = [math.prod(widths[:j]) for j in range(stages)]
    digits = [(me // bases[j]) % widths[j] for j in range(stages)]
    partners = [
        [me + ((digits[j] + d) % widths[j] - digits[j]) * bases[j] for d in range(1, widths[j])]
        for j in range(stages)
    ]
    plans = [list(range(stages)), [0] + list(range(2, stages)) + ([1] if stages > 1 else [])]
    orders = [plans[p] for p in PLANS]

    def size_of(k, s):
        size = n
        for t in range(s):
            size = size // widths[orders[k][t]]
        return size

    def lo_of(k, s):
        lo = 0
        for t in range(s):
            lo = lo + digits[orders[k][t]] * size_of(k, t + 1)
        return lo

    barrier = pltpu.get_barrier_semaphore()
    peers = [peer for group_of in partners for peer in group_of] + [above, below]
    for peer in peers:
        pl.semaphore_signal(barrier, inc=1, device_id={"space": peer}, device_id_type=MESH)

    loads = [
        pltpu.make_async_copy(src, dst, load_sem.at[i])
        for i, (src, dst) in enumerate(
            (
                (off_hbm, off_ref),
                (x_hbm, x_ref),
                (wave_hbm, wavei_ref),
                (charge_hbm, charge_ref),
                (filter_hbm, wfilt_ref),
                (radial_hbm, radial_ref),
            )
        )
    ]
    for load in loads:
        load.start()

    lane = lax.broadcasted_iota(jnp.int32, (1, atoms), 1)
    cell = lane // slots
    held = jnp.zeros((1, atoms), jnp.int32)
    for c in range(cells):
        held = jnp.where(cell == c, counts_ref[c], held)
    live_row = jnp.where(lane % slots < held, 1.0, 0.0).astype(F32)
    cell_x = (cell // GRID).astype(F32)
    cell_y = (cell % GRID).astype(F32)
    loads[0].wait()
    off = jnp.concatenate([off_ref[c].astype(F32) for c in range(cells)], axis=1)
    geo_ref[...] = jnp.concatenate(
        [off, cell_x, cell_y, live_row, jnp.zeros((2, atoms), F32)], axis=0
    )
    placed = jnp.concatenate(
        [
            off,
            cell_x + off[0:1],
            cell_y + off[1:2],
            me.astype(F32) + off[2:3],
            live_row,
            jnp.zeros((1, atoms), F32),
        ],
        axis=0,
    )
    gcol_ref[...] = placed.T
    loads[1].wait()
    masked_ref[...] = (
        x_ref[...].reshape(atoms, feats).astype(F32) * gcol_ref[:, 6:7]
    ).astype(BF16)
    loads[2].wait()
    wave = wavei_ref[...].astype(F32)
    tx, ty, tz = wave[0:1] * (1.0 / GRID), wave[1:2] * (1.0 / GRID), wave[2:3] * (1.0 / n)
    length = (2.0 * math.pi) * jnp.sqrt(tx * tx + ty * ty + tz * tz)
    wave_ref[...] = jnp.concatenate([tx, ty, tz, length, jnp.zeros((4, waves), F32)], axis=0)

    halo = []
    for slot, peer in ((0, above), (1, below)):
        for which, src, dst in ((0, masked_ref, halo_x), (1, geo_ref, halo_geo)):
            copy = pltpu.make_async_remote_copy(
                src_ref=src,
                dst_ref=dst.at[slot],
                send_sem=halo_send.at[slot, which],
                recv_sem=halo_recv.at[slot, which],
                device_id={"space": peer},
                device_id_type=MESH,
            )
            halo.append(copy)

    def scatter_copies(k, s):
        digit = orders[k][s]
        part = size_of(k, s + 1)
        base = n - size_of(k, s)
        return [
            pltpu.make_async_remote_copy(
                src_ref=acc_ref.at[
                    k, pl.ds(lo_of(k, s) + (digits[digit] + d) % widths[digit] * part, part)
                ],
                dst_ref=recv_ref.at[k, pl.ds(base + (d - 1) * part, part)],
                send_sem=send_sem.at[k, s, d - 1],
                recv_sem=recv_sem.at[k, s, d - 1],
                device_id={"space": partners[digit][d - 1]},
                device_id_type=MESH,
            )
            for d in range(1, widths[digit])
        ]

    def gather_copies(k, s):
        digit = orders[k][s]
        part = size_of(k, s + 1)
        place = full_ref.at[k, pl.ds(lo_of(k, s + 1), part)]
        return [
            pltpu.make_async_remote_copy(
                src_ref=place,
                dst_ref=place,
                send_sem=send_sem.at[k, stages + s, d - 1],
                recv_sem=recv_sem.at[k, stages + s, d - 1],
                device_id={"space": partners[digit][d - 1]},
                device_id_type=MESH,
            )
            for d in range(1, widths[digit])
        ]

    def core_copy(k, d):
        digit = orders[k][1]
        part = size_of(k, 2)
        where = (digits[digit] - d + widths[digit]) % widths[digit]
        place = full_ref.at[k, pl.ds(lo_of(k, 1) + where * part, part)]
        return pltpu.make_async_remote_copy(
            src_ref=place,
            dst_ref=place,
            send_sem=send_sem.at[k, stages, d],
            recv_sem=recv_sem.at[k, stages, d],
            device_id={"space": partners[0][0]},
            device_id_type=MESH,
        )

    def start_gather(k, s):
        start_all(gather_copies(k, s))
        if s == 1:
            core_copy(k, 0).start()

    def start_all(copies):
        for copy in copies:
            copy.start()

    def wait_all(copies):
        for copy in copies:
            copy.wait()

    def scatter_finish(k, s):
        wait_all(scatter_copies(k, s))
        part = size_of(k, s + 1)
        keep = lo_of(k, s + 1)
        base = n - size_of(k, s)
        others = widths[orders[k][s]] - 1

        def sum_of(i):
            total = acc_ref[k, keep + i].astype(F32)
            for d in range(others):
                total = total + recv_ref[k, base + d * part + i].astype(F32)
            return total

        if s < stages - 1:

            def add_one(i, carry):
                acc_ref[k, keep + i] = sum_of(i).astype(BF16)
                return carry

            lax.fori_loop(0, part, add_one, 0)
            start_all(scatter_copies(k, s + 1))
        else:
            summed = sum_of(0)
            magnitude = wave_ref[3:4, k * lanes : (k + 1) * lanes]
            weights = filt_ref[keep]
            gain = jnp.zeros((rows, lanes), F32)
            for b in range(basis):
                offset_k = (magnitude - 3.0 * b) * (1.0 / 3.0)
                gain = gain + weights[:, b : b + 1] * jnp.exp(-(offset_k * offset_k))
            full_ref[k, keep] = (summed * gain).astype(BF16)
            start_gather(k, s)

    def inverse(k):
        recip = jnp.zeros((atoms, feats), F32)
        for part, table in ((0, cos_ref), (1, sin_ref)):
            factors = full_ref[k, part * (n // 2) : (part + 1) * (n // 2)].reshape(feats, lanes)
            recip = recip + lax.dot_general(
                table[k], factors, (((1,), (1,)), ((), ())), preferred_element_type=F32
            )
        total_ref[...] = total_ref[...] + recip * scale_recip

    def exchange(k, step):
        if step < stages:
            scatter_finish(k, step)
        else:
            s = 2 * stages - 1 - step
            if s == 0:
                wait_all([core_copy(k, d) for d in range(widths[orders[k][1]])])
            elif s == 1:
                for d, copy in enumerate(gather_copies(k, 1)):
                    copy.wait_recv()
                    core_copy(k, d + 1).start()
                    copy.wait_send()
            else:
                wait_all(gather_copies(k, s))
                start_gather(k, s - 1)

    loads[3].wait()
    charges = jnp.dot(masked_ref[...], charge_ref[...], preferred_element_type=F32)
    charges_t = charges.T.astype(BF16)

    def tables(k, between):
        span = slice(k * lanes, (k + 1) * lanes)

        def table_rows(i, carry):
            at = pl.ds(pl.multiple_of(i * 32, 32), 32)
            turns = (
                gcol_ref[at, 3:4] * wave_ref[0:1, span]
                + gcol_ref[at, 4:5] * wave_ref[1:2, span]
                + gcol_ref[at, 5:6] * wave_ref[2:3, span]
            )
            u = turns - jnp.floor(turns + 0.5)
            sq = u * u
            cos_ref[k, at, :] = poly(COS_TURN, sq).astype(BF16)
            sin_ref[k, at, :] = (u * poly(SIN_TURN, sq)).astype(BF16)
            return carry

        lax.fori_loop(0, atoms // 32, table_rows, 0)
        between()
        real = jnp.dot(charges_t, cos_ref[k], preferred_element_type=F32)
        acc_ref[k, 0 : n // 2] = real.reshape(n // 2, rows, lanes).astype(BF16)
        imag = jnp.dot(charges_t, sin_ref[k], preferred_element_type=F32)
        acc_ref[k, n // 2 : n] = imag.reshape(n // 2, rows, lanes).astype(BF16)
        if k == 0:
            pl.semaphore_wait(barrier, len(peers))
            start_all(halo[1::2])
        start_all(scatter_copies(k, 0))

    def near_values(source, layer):
        for b in range(basis):
            vals_ref[b, layer * atoms : (layer + 1) * atoms, :] = jnp.dot(
                source, radial_ref[b], preferred_element_type=F32
            ).astype(BF16)

    def own_values():
        loads[4].wait()
        loads[5].wait()
        wide = filt_ref.shape[-1]
        weights = jnp.concatenate(
            [wfilt_ref[...], jnp.zeros((wide - basis, feats), F32)], axis=0
        ).T.reshape(n // 2, rows, wide)
        filt_ref[0 : n // 2] = weights
        filt_ref[n // 2 : n] = weights
        near_values(masked_ref[...], 1)

    def halo_places():
        wait_all(halo[1::2])
        near_geo[...] = jnp.concatenate([halo_geo[0], geo_ref[...], halo_geo[1]], axis=1)

    def halo_values():
        wait_all(halo[0::2])
        near_values(halo_x[0], 0)
        near_values(halo_x[1], 2)

    near = 3 * atoms
    mid = basis / 2.0
    group = 16

    def pair_rows(i, carry):
        cell = i // (slots // group)
        start = (i % (slots // group)) * group
        at = pl.ds(pl.multiple_of(i * group, group), group)
        own_x = (cell // GRID).astype(F32)
        own_y = (cell % GRID).astype(F32)
        col = lax.broadcasted_iota(jnp.int32, (1, near), 1)
        shift_x = near_geo[3:4, :] - own_x
        shift_x = jnp.where(shift_x > 1.5, shift_x - GRID, jnp.where(shift_x < -1.5, shift_x + GRID, shift_x))
        shift_y = near_geo[4:5, :] - own_y
        shift_y = jnp.where(shift_y > 1.5, shift_y - GRID, jnp.where(shift_y < -1.5, shift_y + GRID, shift_y))
        shift_z = jnp.where(col < atoms, -1.0, jnp.where(col < 2 * atoms, 0.0, 1.0)).astype(F32)
        dx = (shift_x + near_geo[0:1, :]) - gcol_ref[at, 0:1]
        dy = (shift_y + near_geo[1:2, :]) - gcol_ref[at, 1:2]
        dz = (shift_z + near_geo[2:3, :]) - gcol_ref[at, 2:3]
        sq = dx * dx + dy * dy + dz * dz
        radius = sq * lax.rsqrt(jnp.maximum(sq, 1e-30))
        half_cos = poly(COS_HALF_PI, sq)
        t = jnp.minimum(radius, 1.0) * basis - mid
        row = lax.broadcasted_iota(jnp.int32, (group, near), 0) + start
        itself = (col - (atoms + cell * slots)) == row
        used = (sq < 1.0) & jnp.logical_not(itself)
        core = jnp.where(used, jnp.exp(-(t * t)) * half_cos * half_cos, 0.0)
        grow = jnp.exp(t)
        fall = jnp.exp(-t)
        for b in range(basis):
            d2 = 2 * b + 1 - basis
            weight = core * math.exp(-(d2 * d2) / 4.0)
            if d2 != 0:
                factor = grow if d2 > 0 else fall
                power = factor
                for _ in range(abs(d2) - 1):
                    power = power * factor
                weight = weight * power
            pair_ref[b, at, :] = weight.astype(BF16)
        return carry

    steps = atoms // group

    def pair_span(part, parts):
        lax.fori_loop(part * steps // parts, (part + 1) * steps // parts, pair_rows, 0)

    def short_sum():
        short = jnp.zeros((atoms, feats), F32)
        for b in range(basis):
            short = short + jnp.dot(pair_ref[b], vals_ref[b], preferred_element_type=F32)
        total_ref[...] = short * scale_short

    for k in range(colors):
        tables(k, functools.partial(exchange, k - 1, 0) if k else lambda: None)
    exchange(colors - 1, 0)

    spans = [functools.partial(pair_span, part, PARTS) for part in range(PARTS)]
    tasks = {1: [own_values, halo_places] + spans[:2], 2: spans[2:]}
    tasks[stages] = tasks.get(stages, []) + [halo_values]
    tasks[stages + 1] = tasks.get(stages + 1, []) + [short_sum]
    for step in range(1, 2 * stages):
        if step == 2:
            start_all(halo[0::2])
        for task in tasks.get(step, []):
            task()
        order = range(colors - 1, -1, -1) if step == 1 else range(colors)
        for k in order:
            exchange(k, step)
            if step == 2 * stages - 1:
                inverse(k)

    out_ref[...] = (
        (masked_ref[...].astype(F32) + gcol_ref[:, 6:7] * total_ref[...])
        .astype(BF16)
        .reshape(cells, slots, feats)
    )


def local(atom_features, offsets, counts, radial_weight, charge_weight, wave_filter, wavevectors):
    cells, slots, feats = atom_features.shape
    basis = radial_weight.shape[0]
    waves = wavevectors.shape[1]
    n = lax.axis_size("space")
    power = n.bit_length() - 1
    assert n == 1 << power and power >= 3 and cells == GRID * GRID
    widths = (2,) + (2,) * ((power - 1) % 2) + (4,) * ((power - 1) // 2)
    stages = len(widths)
    atoms = cells * slots
    rows = 2 * feats // n
    colors = len(PLANS)
    lanes = waves // colors
    dims = (
        n,
        widths,
        cells,
        slots,
        feats,
        basis,
        waves,
        1.0 / math.sqrt(slots),
        1.0 / math.sqrt(cells * n * slots * waves),
    )
    anyspace = pl.BlockSpec(memory_space=pl.ANY)
    args = (counts, atom_features, offsets, wavevectors, charge_weight, wave_filter, radial_weight)
    return pl.pallas_call(
        functools.partial(layer_kernel, dims),
        out_shape=jax.ShapeDtypeStruct((cells, slots, feats), BF16),
        in_specs=[pl.BlockSpec(memory_space=pltpu.SMEM)] + [anyspace] * 6,
        out_specs=pl.BlockSpec(memory_space=pltpu.VMEM),
        scratch_shapes=[
            pltpu.VMEM(atom_features.shape, BF16),
            pltpu.VMEM(offsets.shape, BF16),
            pltpu.VMEM(wavevectors.shape, jnp.int32),
            pltpu.VMEM(charge_weight.shape, BF16),
            pltpu.VMEM(wave_filter.shape, F32),
            pltpu.VMEM(radial_weight.shape, BF16),
            pltpu.VMEM((atoms, feats), BF16),
            pltpu.VMEM((8, atoms), F32),
            pltpu.VMEM((atoms, 8), F32),
            pltpu.VMEM((8, waves), F32),
            pltpu.VMEM((n, rows, basis + -basis % 8), F32),
            pltpu.VMEM((2, atoms, feats), BF16),
            pltpu.VMEM((2, 8, atoms), F32),
            pltpu.VMEM((8, 3 * atoms), F32),
            pltpu.VMEM((colors, atoms, lanes), BF16),
            pltpu.VMEM((colors, atoms, lanes), BF16),
            pltpu.VMEM((colors, n, rows, lanes), BF16),
            pltpu.VMEM((colors, n - 1, rows, lanes), BF16),
            pltpu.VMEM((colors, n, rows, lanes), BF16),
            pltpu.VMEM((basis, 3 * atoms, feats), BF16),
            pltpu.VMEM((basis, atoms, 3 * atoms), BF16),
            pltpu.VMEM((atoms, feats), F32),
            pltpu.SemaphoreType.DMA((6,)),
            pltpu.SemaphoreType.DMA((2, 2)),
            pltpu.SemaphoreType.DMA((2, 2)),
            pltpu.SemaphoreType.DMA((colors, 2 * stages, max(widths))),
            pltpu.SemaphoreType.DMA((colors, 2 * stages, max(widths))),
        ],
        compiler_params=pltpu.CompilerParams(collective_id=0, has_side_effects=True),
        name="ewald_layer",
    )(*args)


def solution(mesh):
    in_specs = (
        P(("groups", "space"), None, None),
        P(("groups", "space"), None, None),
        P(("groups", "space")),
        P(),
        P(),
        P(),
        P(),
    )
    out_specs = P(("groups", "space"), None, None)
    return jax.shard_map(local, mesh=mesh, in_specs=in_specs, out_specs=out_specs, check_vma=False)
```

```python
import functools
import math

import jax
import jax.numpy as jnp
from jax import lax
from jax.experimental import pallas as pl
from jax.experimental.pallas import tpu as pltpu
from jax.sharding import PartitionSpec as P

GRID = 3
MESH = pl.DeviceIdType.MESH
PLANS = (1, 0)
PARTS = 4
F32 = jnp.float32
BF16 = jnp.bfloat16

COS_TURN = (
    0.9999999890590222,
    -19.739204499453972,
    64.93911745989816,
    -85.45013953091984,
    60.167630951184535,
    -25.96759924915613,
    6.528658162048644,
)
SIN_TURN = (
    6.283182793407032,
    -41.34141938561698,
    81.59613875538027,
    -76.57968785100171,
    41.20374363359195,
    -12.268859940903283,
)
COS_HALF_PI = tuple((-1) ** i * (math.pi / 2) ** (2 * i) / math.factorial(2 * i) for i in range(7))


def poly(coefs, x):
    total = coefs[-1] * x + coefs[-2]
    for c in coefs[-3::-1]:
        total = total * x + c
    return total


def layer_kernel(
    dims,
    counts_ref,
    x_hbm,
    off_hbm,
    wave_hbm,
    charge_hbm,
    filter_hbm,
    radial_hbm,
    out_ref,
    x_ref,
    off_ref,
    wavei_ref,
    charge_ref,
    wfilt_ref,
    radial_ref,
    masked_ref,
    geo_ref,
    gcol_ref,
    wave_ref,
    filt_ref,
    halo_x,
    halo_geo,
    near_geo,
    cos_ref,
    sin_ref,
    acc_ref,
    recv_ref,
    full_ref,
    vals_ref,
    pair_ref,
    total_ref,
    load_sem,
    halo_send,
    halo_recv,
    send_sem,
    recv_sem,
):
    n, widths, cells, slots, feats, basis, waves, scale_short, scale_recip = dims
    atoms = cells * slots
    rows = 2 * feats // n
    colors = len(PLANS)
    lanes = waves // colors
    me = lax.axis_index("space")
    above, below = lax.rem(me + 1, n), lax.rem(me + n - 1, n)

    stages = len(widths)
    bases = [math.prod(widths[:j]) for j in range(stages)]
    digits = [(me // bases[j]) % widths[j] for j in range(stages)]
    partners = [
        [me + ((digits[j] + d) % widths[j] - digits[j]) * bases[j] for d in range(1, widths[j])]
        for j in range(stages)
    ]
    plans = [list(range(stages)), [0] + list(range(2, stages)) + ([1] if stages > 1 else [])]
    orders = [plans[p] for p in PLANS]

    def size_of(k, s):
        size = n
        for t in range(s):
            size = size // widths[orders[k][t]]
        return size

    def lo_of(k, s):
        lo = 0
        for t in range(s):
            lo = lo + digits[orders[k][t]] * size_of(k, t + 1)
        return lo

    barrier = pltpu.get_barrier_semaphore()
    peers = [peer for group_of in partners for peer in group_of] + [above, below]
    for peer in peers:
        pl.semaphore_signal(barrier, inc=1, device_id={"space": peer}, device_id_type=MESH)

    loads = [
        pltpu.make_async_copy(src, dst, load_sem.at[i])
        for i, (src, dst) in enumerate(
            (
                (off_hbm, off_ref),
                (x_hbm, x_ref),
                (wave_hbm, wavei_ref),
                (charge_hbm, charge_ref),
                (filter_hbm, wfilt_ref),
                (radial_hbm, radial_ref),
            )
        )
    ]
    for load in loads:
        load.start()

    lane = lax.broadcasted_iota(jnp.int32, (1, atoms), 1)
    cell = lane // slots
    held = jnp.zeros((1, atoms), jnp.int32)
    for c in range(cells):
        held = jnp.where(cell == c, counts_ref[c], held)
    live_row = jnp.where(lane % slots < held, 1.0, 0.0).astype(F32)
    cell_x = (cell // GRID).astype(F32)
    cell_y = (cell % GRID).astype(F32)
    loads[0].wait()
    off = jnp.concatenate([off_ref[c].astype(F32) for c in range(cells)], axis=1)
    geo_ref[...] = jnp.concatenate(
        [off, cell_x, cell_y, live_row, jnp.zeros((2, atoms), F32)], axis=0
    )
    placed = jnp.concatenate(
        [
            off,
            cell_x + off[0:1],
            cell_y + off[1:2],
            me.astype(F32) + off[2:3],
            live_row,
            jnp.zeros((1, atoms), F32),
        ],
        axis=0,
    )
    gcol_ref[...] = placed.T
    loads[1].wait()
    masked_ref[...] = (
        x_ref[...].reshape(atoms, feats).astype(F32) * gcol_ref[:, 6:7]
    ).astype(BF16)
    loads[2].wait()
    wave = wavei_ref[...].astype(F32)
    tx, ty, tz = wave[0:1] * (1.0 / GRID), wave[1:2] * (1.0 / GRID), wave[2:3] * (1.0 / n)
    length = (2.0 * math.pi) * jnp.sqrt(tx * tx + ty * ty + tz * tz)
    wave_ref[...] = jnp.concatenate([tx, ty, tz, length, jnp.zeros((4, waves), F32)], axis=0)

    halo = []
    for slot, peer in ((0, above), (1, below)):
        for which, src, dst in ((0, masked_ref, halo_x), (1, geo_ref, halo_geo)):
            copy = pltpu.make_async_remote_copy(
                src_ref=src,
                dst_ref=dst.at[slot],
                send_sem=halo_send.at[slot, which],
                recv_sem=halo_recv.at[slot, which],
                device_id={"space": peer},
                device_id_type=MESH,
            )
            halo.append(copy)

    def scatter_copies(k, s):
        digit = orders[k][s]
        part = size_of(k, s + 1)
        base = n - size_of(k, s)
        return [
            pltpu.make_async_remote_copy(
                src_ref=acc_ref.at[
                    k, pl.ds(lo_of(k, s) + (digits[digit] + d) % widths[digit] * part, part)
                ],
                dst_ref=recv_ref.at[k, pl.ds(base + (d - 1) * part, part)],
                send_sem=send_sem.at[k, s, d - 1],
                recv_sem=recv_sem.at[k, s, d - 1],
                device_id={"space": partners[digit][d - 1]},
                device_id_type=MESH,
            )
            for d in range(1, widths[digit])
        ]

    def gather_copies(k, s):
        digit = orders[k][s]
        part = size_of(k, s + 1)
        place = full_ref.at[k, pl.ds(lo_of(k, s + 1), part)]
        return [
            pltpu.make_async_remote_copy(
                src_ref=place,
                dst_ref=place,
                send_sem=send_sem.at[k, stages + s, d - 1],
                recv_sem=recv_sem.at[k, stages + s, d - 1],
                device_id={"space": partners[digit][d - 1]},
                device_id_type=MESH,
            )
            for d in range(1, widths[digit])
        ]

    def core_copy(k, d):
        digit = orders[k][1]
        part = size_of(k, 2)
        where = (digits[digit] - d + widths[digit]) % widths[digit]
        place = full_ref.at[k, pl.ds(lo_of(k, 1) + where * part, part)]
        return pltpu.make_async_remote_copy(
            src_ref=place,
            dst_ref=place,
            send_sem=send_sem.at[k, stages, d],
            recv_sem=recv_sem.at[k, stages, d],
            device_id={"space": partners[0][0]},
            device_id_type=MESH,
        )

    def start_gather(k, s):
        start_all(gather_copies(k, s))
        if s == 1:
            core_copy(k, 0).start()

    def start_all(copies):
        for copy in copies:
            copy.start()

    def wait_all(copies):
        for copy in copies:
            copy.wait()

    def scatter_finish(k, s):
        wait_all(scatter_copies(k, s))
        part = size_of(k, s + 1)
        keep = lo_of(k, s + 1)
        base = n - size_of(k, s)
        others = widths[orders[k][s]] - 1

        def sum_of(i):
            total = acc_ref[k, keep + i].astype(F32)
            for d in range(others):
                total = total + recv_ref[k, base + d * part + i].astype(F32)
            return total

        if s < stages - 1:

            def add_one(i, carry):
                acc_ref[k, keep + i] = sum_of(i).astype(BF16)
                return carry

            lax.fori_loop(0, part, add_one, 0)
            start_all(scatter_copies(k, s + 1))
        else:
            summed = sum_of(0)
            magnitude = wave_ref[3:4, k * lanes : (k + 1) * lanes]
            weights = filt_ref[keep]
            gain = jnp.zeros((rows, lanes), F32)
            for b in range(basis):
                offset_k = (magnitude - 3.0 * b) * (1.0 / 3.0)
                gain = gain + weights[:, b : b + 1] * jnp.exp(-(offset_k * offset_k))
            full_ref[k, keep] = (summed * gain).astype(BF16)
            start_gather(k, s)

    def inverse(k):
        recip = jnp.zeros((atoms, feats), F32)
        for part, table in ((0, cos_ref), (1, sin_ref)):
            factors = full_ref[k, part * (n // 2) : (part + 1) * (n // 2)].reshape(feats, lanes)
            recip = recip + lax.dot_general(
                table[k], factors, (((1,), (1,)), ((), ())), preferred_element_type=F32
            )
        total_ref[...] = total_ref[...] + recip * scale_recip

    def exchange(k, step):
        if step < stages:
            scatter_finish(k, step)
        else:
            s = 2 * stages - 1 - step
            if s == 0:
                wait_all([core_copy(k, d) for d in range(widths[orders[k][1]])])
            elif s == 1:
                for d, copy in enumerate(gather_copies(k, 1)):
                    copy.wait_recv()
                    core_copy(k, d + 1).start()
                    copy.wait_send()
            else:
                wait_all(gather_copies(k, s))
                start_gather(k, s - 1)

    loads[3].wait()
    charges = jnp.dot(masked_ref[...], charge_ref[...], preferred_element_type=F32)
    charges_t = charges.T.astype(BF16)

    def tables(k, between):
        span = slice(k * lanes, (k + 1) * lanes)

        def table_rows(i, carry):
            at = pl.ds(pl.multiple_of(i * 32, 32), 32)
            turns = (
                gcol_ref[at, 3:4] * wave_ref[0:1, span]
                + gcol_ref[at, 4:5] * wave_ref[1:2, span]
                + gcol_ref[at, 5:6] * wave_ref[2:3, span]
            )
            u = turns - jnp.floor(turns + 0.5)
            sq = u * u
            cos_ref[k, at, :] = poly(COS_TURN, sq).astype(BF16)
            sin_ref[k, at, :] = (u * poly(SIN_TURN, sq)).astype(BF16)
            return carry

        lax.fori_loop(0, atoms // 32, table_rows, 0, unroll=3)
        between()
        real = jnp.dot(charges_t, cos_ref[k], preferred_element_type=F32)
        acc_ref[k, 0 : n // 2] = real.reshape(n // 2, rows, lanes).astype(BF16)
        imag = jnp.dot(charges_t, sin_ref[k], preferred_element_type=F32)
        acc_ref[k, n // 2 : n] = imag.reshape(n // 2, rows, lanes).astype(BF16)
        if k == 0:
            pl.semaphore_wait(barrier, len(peers))
            start_all(halo[1::2])
        start_all(scatter_copies(k, 0))

    def near_values(source, layer):
        for b in range(basis):
            vals_ref[b, layer * atoms : (layer + 1) * atoms, :] = jnp.dot(
                source, radial_ref[b], preferred_element_type=F32
            ).astype(BF16)

    def own_values():
        loads[4].wait()
        loads[5].wait()
        wide = filt_ref.shape[-1]
        weights = jnp.concatenate(
            [wfilt_ref[...], jnp.zeros((wide - basis, feats), F32)], axis=0
        ).T.reshape(n // 2, rows, wide)
        filt_ref[0 : n // 2] = weights
        filt_ref[n // 2 : n] = weights
        near_values(masked_ref[...], 1)

    def halo_places():
        wait_all(halo[1::2])
        near_geo[...] = jnp.concatenate([halo_geo[0], geo_ref[...], halo_geo[1]], axis=1)

    def halo_values():
        wait_all(halo[0::2])
        near_values(halo_x[0], 0)
        near_values(halo_x[1], 2)

    near = 3 * atoms
    mid = basis / 2.0
    group = 16

    def pair_rows(i, carry):
        cell = i // (slots // group)
        start = (i % (slots // group)) * group
        at = pl.ds(pl.multiple_of(i * group, group), group)
        own_x = (cell // GRID).astype(F32)
        own_y = (cell % GRID).astype(F32)
        col = lax.broadcasted_iota(jnp.int32, (1, near), 1)
        shift_x = near_geo[3:4, :] - own_x
        shift_x = jnp.where(shift_x > 1.5, shift_x - GRID, jnp.where(shift_x < -1.5, shift_x + GRID, shift_x))
        shift_y = near_geo[4:5, :] - own_y
        shift_y = jnp.where(shift_y > 1.5, shift_y - GRID, jnp.where(shift_y < -1.5, shift_y + GRID, shift_y))
        shift_z = jnp.where(col < atoms, -1.0, jnp.where(col < 2 * atoms, 0.0, 1.0)).astype(F32)
        dx = (shift_x + near_geo[0:1, :]) - gcol_ref[at, 0:1]
        dy = (shift_y + near_geo[1:2, :]) - gcol_ref[at, 1:2]
        dz = (shift_z + near_geo[2:3, :]) - gcol_ref[at, 2:3]
        sq = dx * dx + dy * dy + dz * dz
        radius = sq * lax.rsqrt(jnp.maximum(sq, 1e-30))
        half_cos = poly(COS_HALF_PI, sq)
        t = jnp.minimum(radius, 1.0) * basis - mid
        row = lax.broadcasted_iota(jnp.int32, (group, near), 0) + start
        itself = (col - (atoms + cell * slots)) == row
        used = (sq < 1.0) & jnp.logical_not(itself)
        core = jnp.where(used, jnp.exp(-(t * t)) * half_cos * half_cos, 0.0)
        grow = jnp.exp(t)
        fall = jnp.exp(-t)
        for b in range(basis):
            d2 = 2 * b + 1 - basis
            weight = core * math.exp(-(d2 * d2) / 4.0)
            if d2 != 0:
                factor = grow if d2 > 0 else fall
                power = factor
                for _ in range(abs(d2) - 1):
                    power = power * factor
                weight = weight * power
            pair_ref[b, at, :] = weight.astype(BF16)
        return carry

    steps = atoms // group

    def pair_span(part, parts):
        lax.fori_loop(part * steps // parts, (part + 1) * steps // parts, pair_rows, 0)

    def short_sum():
        short = jnp.zeros((atoms, feats), F32)
        for b in range(basis):
            short = short + jnp.dot(pair_ref[b], vals_ref[b], preferred_element_type=F32)
        total_ref[...] = short * scale_short

    for k in range(colors):
        tables(k, functools.partial(exchange, k - 1, 0) if k else lambda: None)
    exchange(colors - 1, 0)

    spans = [functools.partial(pair_span, part, PARTS) for part in range(PARTS)]
    tasks = {1: [own_values, halo_places] + spans[:2], 2: spans[2:]}
    tasks[stages] = tasks.get(stages, []) + [halo_values]
    tasks[stages + 1] = tasks.get(stages + 1, []) + [short_sum]
    for step in range(1, 2 * stages):
        if step == 2:
            start_all(halo[0::2])
        for task in tasks.get(step, []):
            task()
        order = range(colors - 1, -1, -1) if step in (1, 2 * stages - 2, 2 * stages - 1) else range(colors)
        for k in order:
            exchange(k, step)
            if step == 2 * stages - 1:
                inverse(k)

    out_ref[...] = (
        (masked_ref[...].astype(F32) + gcol_ref[:, 6:7] * total_ref[...])
        .astype(BF16)
        .reshape(cells, slots, feats)
    )


def local(atom_features, offsets, counts, radial_weight, charge_weight, wave_filter, wavevectors):
    cells, slots, feats = atom_features.shape
    basis = radial_weight.shape[0]
    waves = wavevectors.shape[1]
    n = lax.axis_size("space")
    power = n.bit_length() - 1
    assert n == 1 << power and power >= 3 and cells == GRID * GRID
    widths = (2,) + (2,) * ((power - 1) % 2) + (4,) * ((power - 1) // 2)
    stages = len(widths)
    atoms = cells * slots
    rows = 2 * feats // n
    colors = len(PLANS)
    lanes = waves // colors
    dims = (
        n,
        widths,
        cells,
        slots,
        feats,
        basis,
        waves,
        1.0 / math.sqrt(slots),
        1.0 / math.sqrt(cells * n * slots * waves),
    )
    anyspace = pl.BlockSpec(memory_space=pl.ANY)
    args = (counts, atom_features, offsets, wavevectors, charge_weight, wave_filter, radial_weight)
    return pl.pallas_call(
        functools.partial(layer_kernel, dims),
        out_shape=jax.ShapeDtypeStruct((cells, slots, feats), BF16),
        in_specs=[pl.BlockSpec(memory_space=pltpu.SMEM)] + [anyspace] * 6,
        out_specs=pl.BlockSpec(memory_space=pltpu.VMEM),
        scratch_shapes=[
            pltpu.VMEM(atom_features.shape, BF16),
            pltpu.VMEM(offsets.shape, BF16),
            pltpu.VMEM(wavevectors.shape, jnp.int32),
            pltpu.VMEM(charge_weight.shape, BF16),
            pltpu.VMEM(wave_filter.shape, F32),
            pltpu.VMEM(radial_weight.shape, BF16),
            pltpu.VMEM((atoms, feats), BF16),
            pltpu.VMEM((8, atoms), F32),
            pltpu.VMEM((atoms, 8), F32),
            pltpu.VMEM((8, waves), F32),
            pltpu.VMEM((n, rows, basis + -basis % 8), F32),
            pltpu.VMEM((2, atoms, feats), BF16),
            pltpu.VMEM((2, 8, atoms), F32),
            pltpu.VMEM((8, 3 * atoms), F32),
            pltpu.VMEM((colors, atoms, lanes), BF16),
            pltpu.VMEM((colors, atoms, lanes), BF16),
            pltpu.VMEM((colors, n, rows, lanes), BF16),
            pltpu.VMEM((colors, n - 1, rows, lanes), BF16),
            pltpu.VMEM((colors, n, rows, lanes), BF16),
            pltpu.VMEM((basis, 3 * atoms, feats), BF16),
            pltpu.VMEM((basis, atoms, 3 * atoms), BF16),
            pltpu.VMEM((atoms, feats), F32),
            pltpu.SemaphoreType.DMA((6,)),
            pltpu.SemaphoreType.DMA((2, 2)),
            pltpu.SemaphoreType.DMA((2, 2)),
            pltpu.SemaphoreType.DMA((colors, 2 * stages, max(widths))),
            pltpu.SemaphoreType.DMA((colors, 2 * stages, max(widths))),
        ],
        compiler_params=pltpu.CompilerParams(collective_id=0, has_side_effects=True),
        name="ewald_layer",
    )(*args)


def solution(mesh):
    in_specs = (
        P(("groups", "space"), None, None),
        P(("groups", "space"), None, None),
        P(("groups", "space")),
        P(),
        P(),
        P(),
        P(),
    )
    out_specs = P(("groups", "space"), None, None)
    return jax.shard_map(local, mesh=mesh, in_specs=in_specs, out_specs=out_specs, check_vma=False)
```
